32 devices in a mesh: gx: 2 (over x), gy: 16 (over z, y, core).
Axes of the slice: x: 2, y: 2, z: 4, core: 2. Of those that a mesh axis runs over, the one named last changes fastest.
Arguments:
- snapshot: float32 [19, 64, 4096], P(None, 'gx', 'gy'), may hold values from 0.03 to 0.09
- flags: int32 [64, 4096], P('gx', 'gy'), may hold values from 0 to 3
- porosity: float32 [64, 4096], P('gx', 'gy'), may hold values from 0 to 0.5
- adjoint_end: float32 [19, 64, 4096], P(None, 'gx', 'gy'), may hold values from -12 to 12
Outputs:
- adjoint_start: float32 [19, 64, 4096], P(None, 'gx', 'gy')
- sensitivity: float32 [64, 4096], P('gx', 'gy')
The draws below stay inside these ranges and needn't reach their ends.
Inputs may be any that keep to these rules, and one draw needn't show every extreme that they name: `flags`: 0 marks a fluid cell, 1 a solid wall, 2 an inlet, 3 an outlet.
All inputs are finite; a program needn't handle non-finite values.
Results may differ from the reference program's by a relative error of at most 0.0003.
Values sent between devices are 32-bit elements; how exact they have to be, the bound alone decides.
No kernel may reach another device: no remote copies, remote signals or barrier semaphores. Data moves between devices by JAX's collectives and lax.ppermute only.
A program may use at most 128 MiB of HBM per device.

```python
from functools import partial
import jax
import jax.numpy as jnp
import numpy as np
from jax import lax

Q = 19
NZ = 16
STEPS = 4
NX = 64
NY = 256


def plant(values, own_key, low, largest):
    index_at = [jax.random.randint(jax.random.fold_in(own_key, axis), (), 0, length) for axis, length in enumerate(values.shape)]
    widest = values.shape.index(max(values.shape))
    beside = index_at[:widest] + [(index_at[widest] + 1) % values.shape[widest]] + index_at[widest + 1:]
    return values.at[tuple(index_at)].set(low).at[tuple(beside)].set(largest)


def level_of(key, dims, split, low, top_value):
    factor_of, own = 1.0, jax.random.fold_in(key, 6)
    for axis_at, shards_of in split:
        steps = jnp.exp(jax.random.uniform(jax.random.fold_in(own, axis_at), (shards_of,), jnp.float32, low / len(split), top_value / len(split)))
        factor_of = factor_of * jnp.repeat(steps, dims[axis_at] // shards_of).reshape([-1 if axis == axis_at else 1 for axis in range(len(dims))])
    return factor_of


def gaussian(key, shape, scale, limit, split=(), kind=jnp.bfloat16):
    values = jax.random.normal(key, shape, jnp.float32) * scale
    if len(split) > 0:
        values = level_of(key, shape, split, -0.22, 0.18) * values
    return jnp.clip(values, min=-limit, max=limit).astype(kind)


def setup_inputs(seed: int = 0) -> dict:
    key_of = jax.random.split(jax.random.key(seed), 5)
    return {
        "snapshot": jnp.clip(0.03 + 0.060000004 * jax.random.uniform(key_of[0], (Q, NX, NY * NZ), jnp.float32) ** level_of(key_of[0], (Q, NX, NY * NZ), ((1, 2), (2, 16)), -0.2, 0.2), 0.03, 0.09),
        "flags": plant(jax.random.randint(key_of[1], (NX, NY * NZ), 0, 4), jax.random.fold_in(key_of[1], 1), 0, 3).astype(jnp.int32),
        "porosity": jnp.clip(0.5 * jax.random.uniform(key_of[2], (NX, NY * NZ), jnp.float32) ** level_of(key_of[2], (NX, NY * NZ), ((0, 2), (1, 16)), -0.2, 0.2), 0.0, 0.5),
        "adjoint_end": gaussian(key_of[3], (Q, NX, NY * NZ), 2.0, 12.0, ((1, 2), (2, 16)), jnp.float32),
    }


def lattice_tables():
    velocities = [(0, 0, 0)]
    for axis_pick in range(3):
        for sense in (1, -1):
            vector = [0, 0, 0]
            vector[axis_pick] = sense
            velocities.append(tuple(vector))
    for first_axis, second_axis in ((0, 1), (0, 2), (1, 2)):
        for sense_a in (1, -1):
            for sense_b in (1, -1):
                vector = [0, 0, 0]
                vector[first_axis] = sense_a
                vector[second_axis] = sense_b
                velocities.append(tuple(vector))
    table = np.array(velocities) * 1.0
    weights = np.array([1.0 / 3.0] + [1.0 / 18.0] * 6 + [1.0 / 36.0] * 12)
    opposite = [velocities.index(tuple((-value for value in vector))) for vector in velocities]
    along_x, along_y, along_z = (table[:, 0], table[:, 1], table[:, 2])
    square = along_x ** 2 + along_y ** 2 + along_z ** 2
    basis = [np.ones(19), along_x, along_y, along_z, square, square ** 2, square * along_x, square * along_y, square * along_z, 3 * along_x ** 2 - square, along_y ** 2 - along_z ** 2, along_x * along_y, along_y * along_z, along_x * along_z, square * (3 * along_x ** 2 - square), square * (along_y ** 2 - along_z ** 2), (along_y ** 2 - along_z ** 2) * along_x, (along_z ** 2 - along_x ** 2) * along_y, (along_x ** 2 - along_y ** 2) * along_z]
    ortho = []
    for column in basis:
        vector = np.array(column) * 1.0
        for prior in ortho:
            vector = vector - np.dot(vector, prior) * prior
        vector = vector / np.sqrt(np.dot(vector, vector))
        ortho.append(vector)
    matrix = np.stack(ortho)
    viscous = 1.0 / 0.6
    rates = np.array([0, 0, 0, 0, 1.19, 1.4, 1.2, 1.2, 1.2, viscous, viscous, viscous, viscous, viscous, 1.4, 1.4, 1.98, 1.98, 1.98])
    relax = matrix.T @ (rates[:, None] * matrix)
    inflow = weights * (1 + 0.15 * along_x + 0.01125 * along_x ** 2 - 0.00375)
    return (table, weights, opposite, relax, inflow)

def collide(populations, porosity, flags):
    table, weights, opposite, relax, inflow = lattice_tables()
    lattice = jnp.asarray(table, jnp.float32)
    tail = (1,) * (populations.ndim - 1)
    weight_col = jnp.asarray(weights, jnp.float32).reshape((19,) + tail)
    density = lax.optimization_barrier(jnp.sum(populations, axis=0))
    momentum = jnp.einsum('ia,ixyz->axyz', lattice, populations, precision=lax.Precision.HIGHEST)
    velocity = momentum / density
    projected = jnp.einsum('ia,axyz->ixyz', lattice, velocity, precision=lax.Precision.HIGHEST)
    speed_sq = lax.optimization_barrier(jnp.sum(velocity * velocity, axis=0))
    equilibrium = weight_col * density * (1.0 + 3.0 * projected + 4.5 * projected * projected - 1.5 * speed_sq)
    relaxed = populations - jnp.einsum('ij,jxyz->ixyz', jnp.asarray(relax, jnp.float32), populations - equilibrium, precision=lax.Precision.HIGHEST)
    reflected = jnp.stack([populations[member] for member in opposite])
    inlet = jnp.asarray(inflow, jnp.float32).reshape((19,) + tail)
    base = jnp.where(flags == 0, relaxed, jnp.where(flags == 1, reflected, jnp.where(flags == 2, inlet, equilibrium)))
    return (1.0 - porosity) * base + porosity * reflected

def pull_planes(padded, post, orientation):
    table, weights, opposite, relax, inflow = lattice_tables()
    extent_x, extent_y, extent_z = (post.shape[1], post.shape[2], post.shape[3])
    z_layer = lax.broadcasted_iota(jnp.int32, (extent_x, extent_y, extent_z), 2)
    result = []
    for member in range(19):
        step_x = orientation * int(table[member, 0])
        step_y = orientation * int(table[member, 1])
        step_z = orientation * int(table[member, 2])
        start_x = 1 - step_x
        start_y = 1 - step_y
        source_plane = padded[member, start_x:start_x + extent_x, start_y:start_y + extent_y, :]
        if step_z == 1:
            arrived = jnp.concatenate([jnp.zeros_like(source_plane[:, :, :1]), source_plane[:, :, :-1]], axis=2)
            arrived = jnp.where(z_layer == 0, post[opposite[member]], arrived)
        elif step_z == -1:
            arrived = jnp.concatenate([source_plane[:, :, 1:], jnp.zeros_like(source_plane[:, :, :1])], axis=2)
            arrived = jnp.where(z_layer == extent_z - 1, post[opposite[member]], arrived)
        else:
            arrived = source_plane
        result.append(arrived)
    return jnp.stack(result)

def wrap_pad(field):
    return jnp.pad(field, ((0, 0), (1, 1), (1, 1), (0, 0)), mode='wrap')

def reference(snapshot, flags, porosity, adjoint_end):
    full_shape = (19, NX, NY, NZ)
    populations = snapshot.reshape(full_shape)
    kinds = flags.reshape(full_shape[1:])
    solid_share = porosity.reshape(full_shape[1:])
    stored = []
    for section in range(STEPS):
        stored.append(populations)
        if section + 1 < STEPS:
            post = collide(populations, solid_share, kinds)
            populations = pull_planes(wrap_pad(post), post, 1)
    adjoint = adjoint_end.reshape(full_shape)
    sensitivity = jnp.zeros(full_shape[1:], jnp.float32)
    for section in range(STEPS - 1, -1, -1):
        incoming = pull_planes(wrap_pad(adjoint), adjoint, -1)
        primal, backward = jax.vjp(partial(collide, flags=kinds), stored[section], solid_share)
        adjoint, share_grad = backward(incoming)
        sensitivity = sensitivity + share_grad
    return (adjoint.reshape(19, NX, NY * NZ), sensitivity.reshape(NX, NY * NZ))
```

```python
import jax
import jax.numpy as jnp
from jax import lax
from jax.experimental import pallas as pl
from jax.experimental.pallas import tpu as pltpu
from jax.sharding import PartitionSpec as P

NZ = 16
LANES = 128
F32 = jnp.float32


def velocity_list():
    found = [(0, 0, 0)]
    for axis in range(3):
        for sense in (1, -1):
            vector = [0, 0, 0]
            vector[axis] = sense
            found.append(tuple(vector))
    for a, b in ((0, 1), (0, 2), (1, 2)):
        for sense_a in (1, -1):
            for sense_b in (1, -1):
                vector = [0, 0, 0]
                vector[a], vector[b] = sense_a, sense_b
                found.append(tuple(vector))
    return found


VEL = velocity_list()
OPP = [VEL.index(tuple(-v for v in c)) for c in VEL]
PAIRS = [(1, 2), (3, 4), (5, 6), (7, 10), (8, 9), (11, 14), (12, 13), (15, 18), (16, 17)]
R_E, R_EPS, R_Q, R_NU, R_PI, R_M = 1.19, 1.4, 1.2, 1.0 / 0.6, 1.4, 1.98
WALL = (11, 15)
IN_CX, IN_NO = 1 + 0.01125 - 0.00375, 1 - 0.00375


def cell_kinds(kind):
    fluid, outlet, inlet, wall = kind == 0.0, kind == 3.0, kind == 2.0, kind == 1.0

    def rate(value, scale):
        return jnp.where(fluid, value * scale, jnp.where(outlet, scale, 0.0)).astype(F32)

    turn = jnp.where(wall, 0.0, jnp.where(inlet, 1.0, 2.0)).astype(F32)
    return inlet, turn, rate


def moments(f):
    s = [f[a] + f[b] for a, b in PAIRS]
    d = [f[a] - f[b] for a, b in PAIRS]
    big_s = [s[3] + s[4], s[5] + s[6], s[7] + s[8]]
    off = [s[3] - s[4], s[5] - s[6], s[7] - s[8]]
    ex, gy = d[3] + d[4], d[3] - d[4]
    gx, ez = d[5] + d[6], d[5] - d[6]
    ey, gz = d[7] + d[8], d[7] - d[8]
    return s, d, big_s, off, (ex, ey, ez), (gx, gy, gz)


def spread(e1, e2, a1, b1, a2, b2, t, q, m):
    zero = 12.0 * e2 - 30.0 * e1
    axis = -22.0 * e1 - 8.0 * e2
    edge = 16.0 * e1 + 2.0 * e2
    xy, xz, yz = edge + b1 + b2, edge + b1 - b2, edge - 2.0 * b1
    sums = [
        axis + 2.0 * a1, axis - a1 + a2, axis - a1 - a2,
        xy + t[0], xy - t[0], xz + t[1], xz - t[1], yz + t[2], yz - t[2],
    ]
    return zero, sums


def odd_terms(q, m, j):
    if j is None:
        along = [-4.0 * q[a] for a in range(3)]
        pos = [q[a] + m[a] for a in range(3)]
        neg = [q[a] - m[a] for a in range(3)]
    else:
        along = [-4.0 * q[a] - j[a] for a in range(3)]
        base = [q[a] - j[a] for a in range(3)]
        pos = [base[a] + m[a] for a in range(3)]
        neg = [base[a] - m[a] for a in range(3)]
    return along + [
        pos[0] + neg[1], pos[0] - neg[1], neg[0] + pos[2], neg[0] - pos[2], pos[1] + neg[2], pos[1] - neg[2],
    ]


def collide_tile(f, kind, porous, want_post=True):
    inlet, turn, rate = cell_kinds(kind)
    s, d, big, off, e, g = moments(f)
    axis_sum = s[0] + s[1] + s[2]
    edge_sum = big[0] + big[1] + big[2]
    rho = f[0] + axis_sum + edge_sum
    eg = [e[a] + g[a] for a in range(3)]
    j = [d[a] + eg[a] for a in range(3)]
    inv = 1.0 / rho
    u = [j[a] * inv for a in range(3)]
    xx, yy, zz = j[0] * u[0], j[1] * u[1], j[2] * u[2]
    energy = xx + yy + zz
    e1 = rate(R_E, 1 / 126) * (edge_sum - f[0] - energy)
    r_eps = rate(R_EPS, 1.0)
    e2 = (r_eps * (1 / 252)) * (9.0 * f[0] - 7.0 * axis_sum - 2.0 * edge_sum + 5.5 * energy)
    r_nu = rate(R_NU, 1.0)
    yz_a, yz_e, yz_u = s[1] - s[2], big[0] - big[1], yy - zz
    x_a = 2.0 * s[0] - (s[1] + s[2])
    x_e = big[0] + big[1] - 2.0 * big[2]
    x_u = 2.0 * xx - (yy + zz)
    p1 = (r_nu * (1 / 18)) * (x_a + x_e - x_u)
    q1 = (r_eps * (1 / 36)) * (x_e - 2.0 * x_a + 0.5 * x_u)
    p2 = (r_nu * (1 / 6)) * (yz_a + yz_e - yz_u)
    q2 = (r_eps * (1 / 12)) * (yz_e - 2.0 * yz_a + 0.5 * yz_u)
    half_nu = r_nu * 0.5
    t = [half_nu * (off[0] - j[0] * u[1]), half_nu * (off[1] - j[0] * u[2]), half_nu * (off[2] - j[1] * u[2])]
    r_q, r_m = rate(R_Q, 1 / 12), rate(R_M, 1 / 4)
    q = [r_q * (eg[a] - 2.0 * d[a]) for a in range(3)]
    m = [r_m * (e[a] - g[a]) for a in range(3)]
    zero, sums = spread(e1, e2, p1 - 2.0 * q1, p1 + q1, p2 - 2.0 * q2, p2 + q2, t, q, m)
    diffs = odd_terms(q, m, None)
    gap0 = jnp.where(inlet, f[0] - IN_NO / 3, zero)
    gap = [None] * 19
    gap[0] = gap0
    post = [None] * 19
    share = 1.0 - porous
    half = 0.5 * share
    if want_post:
        post[0] = f[0] - share * gap0
    for n, (a, b) in enumerate(PAIRS):
        weight = (1 / 9 if n < 3 else 1 / 18)
        has_x = VEL[a][0] != 0
        in_s = weight * (IN_CX if has_x else IN_NO)
        in_d = weight * 0.15 if has_x else 0.0
        gs = jnp.where(inlet, s[n] - in_s, sums[n])
        gd = diffs[n] - turn * d[n]
        if has_x:
            gd = jnp.where(inlet, gd - in_d, gd)
        gap[a], gap[b] = gs + gd, gs - gd
        if want_post:
            post[a] = f[b] - half * gap[a]
            post[b] = f[a] - half * gap[b]
    return post, u, gap


def adjoint_tile(b, u, kind, porous):
    inlet, turn, rate = cell_kinds(kind)
    s, d, big, off, e, g = moments(b)
    axis_sum = s[0] + s[1] + s[2]
    edge_sum = big[0] + big[1] + big[2]
    eg = [e[a] + g[a] for a in range(3)]
    e1 = rate(R_E, 1 / 2394) * (8.0 * edge_sum - 11.0 * axis_sum - 30.0 * b[0])
    r_eps = rate(R_EPS, 1.0)
    e2 = (r_eps * (1 / 252)) * (12.0 * b[0] - 4.0 * axis_sum + edge_sum)
    r_nu = rate(R_NU, 1.0)
    yz_a, yz_e = s[1] - s[2], big[0] - big[1]
    x_a = 2.0 * s[0] - (s[1] + s[2])
    x_e = big[0] + big[1] - 2.0 * big[2]
    p1 = (r_nu * (1 / 18)) * (x_a + x_e)
    q1 = (r_eps * (1 / 36)) * (x_e - 2.0 * x_a)
    p2 = (r_nu * (1 / 6)) * (yz_a + yz_e)
    q2 = (r_eps * (1 / 12)) * (yz_e - 2.0 * yz_a)
    half_nu = r_nu * 0.5
    t = [half_nu * off[n] for n in range(3)]
    r_q, r_m = rate(R_Q, 1 / 20), rate(R_M, 1 / 4)
    q = [r_q * (eg[a] - 4.0 * d[a]) for a in range(3)]
    m = [r_m * (e[a] - g[a]) for a in range(3)]
    common = 38.0 * e1 - 11.0 * e2
    v = p1 - 0.5 * q1
    w = p2 - 0.5 * q2
    k = [common + 2.0 * v, common - v + w, common - v - w]
    k2 = [k[a] + k[a] for a in range(3)]
    gx = k2[0] * u[0] + t[0] * u[1] + t[1] * u[2]
    gy = k2[1] * u[1] + t[0] * u[0] + t[2] * u[2]
    gz = k2[2] * u[2] + t[1] * u[0] + t[2] * u[1]
    quad = 0.5 * (gx * u[0] + gy * u[1] + gz * u[2])
    by_rho = 6.0 * e2 - 22.0 * e1 - quad
    by_j = [gx - (2 / 3) * q[0], gy - (2 / 3) * q[1], gz - (2 / 3) * q[2]]
    zero, sums = spread(e1, e2, p1 - 2.0 * q1, p1 + q1, p2 - 2.0 * q2, p2 + q2, t, q, m)
    diffs = odd_terms(q, m, by_j)
    zero = zero - 0.5 * by_rho
    share = 1.0 - porous
    half = 0.5 * share
    out = [None] * 19
    out[0] = b[0] - share * jnp.where(inlet, b[0], zero)
    for n, (a, c) in enumerate(PAIRS):
        gs = jnp.where(inlet, s[n], sums[n] - by_rho)
        gd = diffs[n] - turn * d[n]
        out[a] = b[c] - half * (gs + gd)
        out[c] = b[a] - half * (gs - gd)
    return out


def dot_gap(b, gap):
    total = (b[1] * gap[1] + b[2] * gap[2]) + (b[3] * gap[3] + b[4] * gap[4])
    for i in range(5, 19):
        total = total + b[i] * gap[i]
    return b[0] * gap[0] + 0.5 * total


def iota(axis):
    return lax.broadcasted_iota(jnp.int32, (8, LANES), axis)


def pull(load, lane, sense, columns, column, base=0):
    z = lane & (NZ - 1)
    arrived = []
    for i, (cx, cy, cz) in enumerate(VEL):
        shift = sense * (NZ * cy + cz) - base
        step_z = sense * cz

        def shifted(plane, off_x, amount):
            here = load(plane, column, off_x)
            if amount == 0:
                return here
            other = column - 1 if amount > 0 else column + 1
            if columns and columns > 0:
                other %= columns
            elif base == 0 and not 0 <= other < 3:
                return pltpu.roll(here, amount % LANES, 1)
            there = load(plane, other, off_x)
            if amount > 0:
                mixed = jnp.where(lane >= LANES - amount, there, here)
            else:
                mixed = jnp.where(lane < -amount, there, here)
            return pltpu.roll(mixed, amount % LANES, 1)

        value = shifted(i, -sense * cx, shift)
        if step_z != 0:
            own = shifted(OPP[i], 0, -base)
            value = jnp.where(z == (0 if step_z == 1 else NZ - 1), own, value)
        arrived.append(value)
    return arrived


def counts(c):
    return (5 - c, 3 + c), (5 + c, 3 - c)


def first_kernel(snap_ref, flag_ref, por_ref, adj_ref, post_ref, u_ref, gap_ref, xp_ref, out_ref, in_ref, dg_ref):
    core = lax.rem(lax.axis_index("gy"), 2)
    rows = snap_ref.shape[1]
    lane, row = iota(1), iota(0)
    for c in range(2):
        lanes = slice(c * LANES, (c + 1) * LANES)

        def tile(g, carry):
            at = pl.ds(pl.multiple_of(g * 8, 8), 8)
            f = [snap_ref[i, at, lanes] for i in range(19)]
            post, u, gap = collide_tile(f, flag_ref[at, lanes].astype(F32), por_ref[at, lanes])
            for i in range(19):
                post_ref[i, at, lanes] = post[i]
                gap_ref[i, at, lanes] = gap[i]
            for a in range(3):
                u_ref[a, at, lanes] = u[a]
            return carry

        lax.fori_loop(0, rows // 8, tile, 0)

    def plane(i, at, lanes):
        if i < 19:
            return post_ref[i, at, lanes]
        return por_ref[at, lanes] if i == 19 else flag_ref[at, lanes].astype(F32)

    def low_spare(i, at, lanes, axis, where, unit, roll):
        value, first = plane(i, at, lanes), WALL[axis]
        extras = [(post_ref, 0, 4, 5), (post_ref, 1, 4, 6), (adj_ref, 2, 2, 7)] if i == 19 else [(adj_ref, 3, 2, 5)]
        for ref, n, layer, slot in extras:
            moved = roll(ref[first + n, at, lanes], unit * (slot - layer))
            value = jnp.where(where >= unit * slot, moved, value)
        return value

    def high_spare(i, at, lanes, axis, where, unit, roll):
        value, first = plane(i, at, lanes), WALL[axis]
        extras = [(post_ref, 2, 3, 2), (adj_ref, 1, 5, 1), (adj_ref, 0, 5, 0)] if i == 19 else [(post_ref, 3, 3, 2)]
        for ref, n, layer, slot in extras:
            moved = roll(ref[first + n, at, lanes], (unit * (slot - layer)) % (unit * 8))
            value = jnp.where(where < unit * (slot + 1), moved, value)
        return value

    def roll_rows(value, amount):
        return pltpu.roll(value, amount, 0)

    def roll_lanes(value, amount):
        return pltpu.roll(value, amount, 1)

    low_rows, high_rows = slice(0, 8), slice(rows - 8, rows)
    for c in range(2):
        lanes = slice(c * LANES, (c + 1) * LANES)
        for i in range(21):
            low, high = plane(i, low_rows, lanes), plane(i, high_rows, lanes)
            if i < 19:
                (n_low, _), (_, m_high) = counts(VEL[i][0])
                low = jnp.where(row < n_low, low, pltpu.roll(adj_ref[i, low_rows, lanes], n_low, 0))
                high = jnp.where(row >= m_high, high, pltpu.roll(adj_ref[i, high_rows, lanes], m_high, 0))
            else:
                low = low_spare(i, low_rows, lanes, 0, row, 1, roll_rows)
                high = high_spare(i, high_rows, lanes, 0, row, 1, roll_rows)
            xp_ref[0, i, :, lanes] = low
            xp_ref[1, i, :, lanes] = high

            @pl.when(core == c)
            def _():
                dg_ref[0, i] = low
                dg_ref[1, i] = high

    def pack_low(dst):
        for i in range(21):
            for g in range(rows // 8):
                at = slice(8 * g, 8 * g + 8)
                value = plane(i, at, slice(0, LANES))
                if i < 19:
                    (n, _), _ = counts(VEL[i][1])
                    value = jnp.where(lane < NZ * n, value, pltpu.roll(adj_ref[i, at, slice(0, LANES)], NZ * n, 1))
                else:
                    value = low_spare(i, at, slice(0, LANES), 1, lane, NZ, roll_lanes)
                dst[i, at, :] = value

    def pack_high(dst):
        for i in range(21):
            for g in range(rows // 8):
                at = slice(8 * g, 8 * g + 8)
                value = plane(i, at, slice(LANES, 2 * LANES))
                if i < 19:
                    _, (_, m) = counts(VEL[i][1])
                    value = jnp.where(lane >= NZ * m, value, pltpu.roll(adj_ref[i, at, slice(LANES, 2 * LANES)], NZ * m, 1))
                else:
                    value = high_spare(i, at, slice(LANES, 2 * LANES), 1, lane, NZ, roll_lanes)
                dst[i, at, :] = value

    @pl.when(core == 0)
    def _():
        pack_low(out_ref)
        pack_high(in_ref)

    @pl.when(core == 1)
    def _():
        pack_low(in_ref)
        pack_high(out_ref)


def second_kernel(
    post_hbm, adj_hbm, u0_hbm, gap0_hbm, por_ref, flag_ref, xr_hbm, out_hbm, in_hbm, dg_hbm, xin_hbm,
    res_ref, sens_ref,
    post_in, adj_in, u0_ref, gap0_ref, xr, yr, xy, sems,
    p0, p1, p2, pf, u1, u2, u3, g1, g2, g3, a4, a3, a2, a1, s1, s2, s3,
):
    core = lax.rem(lax.axis_index("gy"), 2)
    rows = por_ref.shape[0]
    groups = rows // 8
    copies = [
        (post_hbm, post_in), (adj_hbm, adj_in), (out_hbm, yr.at[core]), (in_hbm, yr.at[1 - core]), (xr_hbm, xr),
        (dg_hbm, xy.at[core]), (xin_hbm.at[:, :, :, pl.ds(pl.multiple_of(core * LANES, LANES), LANES)], xy.at[1 - core]),
        (u0_hbm, u0_ref), (gap0_hbm, gap0_ref),
    ]
    copies = [pltpu.make_async_copy(src, dst, sems.at[n]) for n, (src, dst) in enumerate(copies)]
    for copy in copies:
        copy.start()
    lane = iota(1)
    upper = lane >= 64

    def ring(low, first, second, high, wide):
        picks = [(low, first), (first, second), (second, high)] + ([(high, low)] if wide else [])
        return [pltpu.roll(jnp.where(upper, a, b), 64, 1) for a, b in picks]

    for copy in copies[:4]:
        copy.wait()
    for i in range(21):
        for g in range(groups):
            at = slice(8 * g, 8 * g + 8)
            low, high = yr[0, i, at], yr[1, i, at]
            if i < 19:
                first, second = post_in[i, at, 0:LANES], post_in[i, at, LANES:]
                dst = p0
            else:
                src = por_ref if i == 19 else flag_ref
                first, second = src[at, 0:LANES].astype(F32), src[at, LANES:].astype(F32)
                dst = pf
            spare = i - WALL[1]
            low_now, high_now = low, high
            if spare in (0, 1):
                high_now = jnp.where(upper, pltpu.roll(yr[1, 19, at], (NZ * (4 - 5 - spare)) % LANES, 1), high)
            if spare in (2, 3):
                low_now = jnp.where(upper, low, pltpu.roll(yr[0, 17 + spare, at], NZ, 1))
            for c, value in enumerate(ring(low_now, first, second, high_now, True)):
                dst[i % 19, c, 6 + 8 * g : 14 + 8 * g] = value
            if i < 19:
                (n, _), (_, m) = counts(VEL[i][1])
                low = pltpu.roll(low, LANES - NZ * m, 1)
                high = pltpu.roll(high, LANES - NZ * n, 1)
                if spare in (0, 1):
                    low = jnp.where(lane >= 96, low, pltpu.roll(yr[0, 19, at], NZ * (5 - spare), 1))
                if spare in (2, 3):
                    away = (7, 5)[spare - 2]
                    high = jnp.where(lane < 32, high, pltpu.roll(yr[1, 17 + spare, at], LANES - NZ * (away - 2), 1))
                for c, value in enumerate(ring(low, adj_in[i, at, 0:LANES], adj_in[i, at, LANES:], high, False)):
                    a4[i, c, 4 + 8 * g : 12 + 8 * g] = value
    for copy in copies[4:7]:
        copy.wait()
    for i in range(21):
        tile = ring(xy[0, 0, i], xr[0, i, :, 0:LANES], xr[0, i, :, LANES:], xy[1, 0, i], True)
        (n, m), _ = counts(VEL[i][0] if i < 19 else 0)
        for c in range(4):
            if i < 19:
                p0[i, c, 6 + rows : 6 + rows + n] = tile[c][0:n]
                if c < 3:
                    a4[i, c, 4 + rows : 4 + rows + m] = tile[c][n:8]
            else:
                pf[i - 19, c, 6 + rows : 14 + rows] = tile[c]
                for dst, n, base, layer, slot in ((p0, 0, 6, 4, 5), (p0, 1, 6, 4, 6), (a4, 2, 4, 2, 7)) if i == 19 else ((a4, 3, 4, 2, 5),):
                    if dst is p0 or c < 3:
                        at = base + rows + layer
                        dst[WALL[0] + n, c, at : at + 1] = tile[c][slot : slot + 1]
        tile = ring(xy[0, 1, i], xr[1, i, :, 0:LANES], xr[1, i, :, LANES:], xy[1, 1, i], True)
        _, (n, m) = counts(VEL[i][0] if i < 19 else 0)
        for c in range(4):
            if i < 19:
                p0[i, c, 6 - n : 6] = tile[c][8 - n : 8]
                if c < 3:
                    a4[i, c, 4 - m : 4] = tile[c][0:m]
            else:
                pf[i - 19, c, 0:6] = tile[c][2:8]
                for dst, n, slot in ((a4, 0, 0), (a4, 1, 1), (p0, 2, 2)) if i == 19 else ((p0, 3, 2),):
                    if dst is p0 or c < 3:
                        dst[WALL[0] + n, c, 1:2] = tile[c][slot : slot + 1]

    def forward(src, src_base, base, n_groups, n_cols, ring_cols, post_dst, u_dst, gap_dst):
        def body(k, carry):
            def load(i, c, off):
                return src[i, c, pl.ds(8 * k + (base - src_base + off), 8)]

            at = pl.ds(pl.multiple_of(8 * k, 8), 8)
            for c in range(n_cols):
                f = pull(load, lane, 1, ring_cols, c)
                cells = pl.ds(8 * k + (base + 6), 8)
                post, u, gap = collide_tile(f, pf[1, c, cells], pf[0, c, cells], post_dst is not None)
                if post_dst is not None:
                    for i in range(19):
                        post_dst[i, c, at] = post[i]
                if c < 3:
                    for a in range(3):
                        u_dst[a, c, at] = u[a]
                    for i in range(19):
                        gap_dst[i, c, at] = gap[i]
            return carry

        lax.fori_loop(0, n_groups, body, 0)

    forward(p0, -6, -5, groups + 2, 4, 4, p1, u1, g1)
    forward(p1, -5, -4, groups + 1, 3, 4, p2, u2, g2)
    forward(p2, -4, -3, groups + 1, 3, 0, None, u3, g3)

    def backward(src, src_base, base, dst, u_src, gap_src, f_base, s_dst):
        def body(k, carry):
            def load(i, c, off):
                return src[i, c, pl.ds(8 * k + (base - src_base + off), 8)]

            at = pl.ds(pl.multiple_of(8 * k, 8), 8)
            cells = pl.ds(8 * k + (base + 6), 8)
            old = pl.ds(8 * k + (base - f_base), 8)
            for c in range(3):
                b = pull(load, lane, -1, 0, c)
                s_dst[c, at] = dot_gap(b, [gap_src[i, c, old] for i in range(19)])
                a = adjoint_tile(b, [u_src[n, c, old] for n in range(3)], pf[1, c, cells], pf[0, c, cells])
                for i in range(19):
                    dst[i, c, at] = a[i]
            return carry

        lax.fori_loop(0, groups + 1, body, 0)

    backward(a4, -4, -3, a3, u3, g3, -3, s3)
    backward(a3, -3, -2, a2, u2, g2, -4, s2)
    backward(a2, -2, -1, a1, u1, g1, -5, s1)

    for copy in copies[7:]:
        copy.wait()

    def last(k, carry):
        at = pl.ds(pl.multiple_of(8 * k, 8), 8)

        def load(i, c, off):
            return a1[i, c, pl.ds(8 * k + (1 + off), 8)]

        for c in range(2):
            lanes = slice(c * LANES, (c + 1) * LANES)
            b = pull(load, lane, -1, -1, c, 64)
            total = dot_gap(b, [gap0_ref[i, at, lanes] for i in range(19)])
            parts = []
            for col in (c, c + 1):
                parts.append(
                    s3[col, pl.ds(8 * k + 3, 8)] + s2[col, pl.ds(8 * k + 2, 8)] + s1[col, pl.ds(8 * k + 1, 8)]
                )
            sens_ref[at, lanes] = total + pltpu.roll(jnp.where(upper, parts[0], parts[1]), 64, 1)
            a = adjoint_tile(b, [u0_ref[n, at, lanes] for n in range(3)], flag_ref[at, lanes].astype(F32), por_ref[at, lanes])
            for i in range(19):
                res_ref[i, at, lanes] = a[i]
        return carry

    lax.fori_loop(0, groups, last, 0)


VMEM = pl.BlockSpec(memory_space=pltpu.VMEM)
ANY = pl.BlockSpec(memory_space=pl.ANY)


def exchange(xp, out, inside, dg):
    nx, ny = lax.axis_size("gx"), lax.axis_size("gy")
    same = [(i, i ^ 1) for i in range(ny)]
    other = [(i, (i + 1) % ny if i % 2 else (i - 1) % ny) for i in range(ny)]

    def along(value, axes, pairs_of):
        if nx == 2:
            return lax.ppermute(value, axes, pairs_of(1))
        return jnp.stack([lax.ppermute(value[0], axes, pairs_of(-1)), lax.ppermute(value[1], axes, pairs_of(1))])

    xr = along(xp, "gx", lambda step: [(i, (i + step) % nx) for i in range(nx)])
    out_r = lax.ppermute(out, "gy", other)
    dg_r = along(
        dg, ("gx", "gy"), lambda step: [(i * ny + j, ((i + step) % nx) * ny + k) for i in range(nx) for j, k in other]
    )
    in_r = lax.ppermute(inside, "gy", same)
    xr, out_r, dg_r, in_r = lax.optimization_barrier((xr, out_r, dg_r, in_r))
    xin = lax.ppermute(xr, "gy", same)
    return xr, out_r, in_r, dg_r, xin


def per_device(snapshot, flags, porosity, adjoint_end):
    _, rows, lanes = snapshot.shape
    assert lanes == 2 * LANES and rows % 8 == 0

    def array(*shape):
        return jax.ShapeDtypeStruct(shape, F32)

    post, u0, gap0, xp, out, inside, dg = pl.pallas_call(
        first_kernel,
        out_shape=(
            array(19, rows, lanes), array(3, rows, lanes), array(19, rows, lanes), array(2, 21, 8, lanes),
            array(21, rows, LANES), array(21, rows, LANES), array(2, 21, 8, LANES),
        ),
        in_specs=[VMEM] * 4,
        out_specs=(VMEM,) * 7,
        compiler_params=pltpu.CompilerParams(vmem_limit_bytes=48 << 20),
        name="collide_and_pack",
    )(snapshot, flags, porosity, adjoint_end)
    received = exchange(xp, out, inside, dg)
    tall, mid = rows + 24, rows + 16

    def scratch(*shape):
        return pltpu.VMEM(shape, F32)

    return pl.pallas_call(
        second_kernel,
        out_shape=(array(19, rows, lanes), array(rows, lanes)),
        in_specs=[ANY] * 4 + [VMEM] * 2 + [ANY] * 5,
        out_specs=(VMEM, VMEM),
        scratch_shapes=[
            scratch(19, rows, lanes), scratch(19, rows, lanes), scratch(3, rows, lanes), scratch(19, rows, lanes),
            scratch(2, 21, 8, lanes), scratch(2, 21, rows, LANES), scratch(2, 2, 21, 8, LANES),
            pltpu.SemaphoreType.DMA((9,)),
            scratch(19, 4, tall, LANES), scratch(19, 4, tall, LANES), scratch(19, 3, tall, LANES), scratch(2, 4, tall, LANES),
            scratch(3, 3, mid, LANES), scratch(3, 3, mid, LANES), scratch(3, 3, mid, LANES),
            scratch(19, 3, mid, LANES), scratch(19, 3, mid, LANES), scratch(19, 3, mid, LANES),
            scratch(19, 3, mid, LANES), scratch(19, 3, mid, LANES), scratch(19, 3, mid, LANES), scratch(19, 3, mid, LANES),
            scratch(3, mid, LANES), scratch(3, mid, LANES), scratch(3, mid, LANES),
        ],
        compiler_params=pltpu.CompilerParams(vmem_limit_bytes=56 << 20),
        name="window",
    )(post, adjoint_end, u0, gap0, porosity, flags, *received)


def solution(mesh):
    placed = (P(None, "gx", "gy"), P("gx", "gy"), P("gx", "gy"), P(None, "gx", "gy"))
    return jax.shard_map(
        per_device,
        mesh=mesh,
        in_specs=placed,
        out_specs=(P(None, "gx", "gy"), P("gx", "gy")),
        check_vma=False,
    )
```

```python
import jax
import jax.numpy as jnp
from jax import lax
from jax.experimental import pallas as pl
from jax.experimental.pallas import tpu as pltpu
from jax.sharding import PartitionSpec as P

NZ = 16
LANES = 128
F32 = jnp.float32


def velocity_list():
    found = [(0, 0, 0)]
    for axis in range(3):
        for sense in (1, -1):
            vector = [0, 0, 0]
            vector[axis] = sense
            found.append(tuple(vector))
    for a, b in ((0, 1), (0, 2), (1, 2)):
        for sense_a in (1, -1):
            for sense_b in (1, -1):
                vector = [0, 0, 0]
                vector[a], vector[b] = sense_a, sense_b
                found.append(tuple(vector))
    return found


VEL = velocity_list()
OPP = [VEL.index(tuple(-v for v in c)) for c in VEL]
PAIRS = [(1, 2), (3, 4), (5, 6), (7, 10), (8, 9), (11, 14), (12, 13), (15, 18), (16, 17)]
R_E, R_EPS, R_Q, R_NU, R_PI, R_M = 1.19, 1.4, 1.2, 1.0 / 0.6, 1.4, 1.98
WALL = (11, 15)
IN_CX, IN_NO = 1 + 0.01125 - 0.00375, 1 - 0.00375


def cell_kinds(kind):
    fluid, outlet, inlet, wall = kind == 0.0, kind == 3.0, kind == 2.0, kind == 1.0

    def rate(value, scale):
        return jnp.where(fluid, value * scale, jnp.where(outlet, scale, 0.0)).astype(F32)

    turn = jnp.where(wall, 0.0, jnp.where(inlet, 1.0, 2.0)).astype(F32)
    return inlet, turn, rate


def moments(f):
    s = [f[a] + f[b] for a, b in PAIRS]
    d = [f[a] - f[b] for a, b in PAIRS]
    big_s = [s[3] + s[4], s[5] + s[6], s[7] + s[8]]
    off = [s[3] - s[4], s[5] - s[6], s[7] - s[8]]
    ex, gy = d[3] + d[4], d[3] - d[4]
    gx, ez = d[5] + d[6], d[5] - d[6]
    ey, gz = d[7] + d[8], d[7] - d[8]
    return s, d, big_s, off, (ex, ey, ez), (gx, gy, gz)


def spread(e1, e2, a1, b1, a2, b2, t, q, m):
    zero = 12.0 * e2 - 30.0 * e1
    axis = -22.0 * e1 - 8.0 * e2
    edge = 16.0 * e1 + 2.0 * e2
    xy, xz, yz = edge + b1 + b2, edge + b1 - b2, edge - 2.0 * b1
    sums = [
        axis + 2.0 * a1, axis - a1 + a2, axis - a1 - a2,
        xy + t[0], xy - t[0], xz + t[1], xz - t[1], yz + t[2], yz - t[2],
    ]
    return zero, sums


def odd_terms(q, m, j):
    if j is None:
        along = [-4.0 * q[a] for a in range(3)]
        pos = [q[a] + m[a] for a in range(3)]
        neg = [q[a] - m[a] for a in range(3)]
    else:
        along = [-4.0 * q[a] - j[a] for a in range(3)]
        base = [q[a] - j[a] for a in range(3)]
        pos = [base[a] + m[a] for a in range(3)]
        neg = [base[a] - m[a] for a in range(3)]
    return along + [
        pos[0] + neg[1], pos[0] - neg[1], neg[0] + pos[2], neg[0] - pos[2], pos[1] + neg[2], pos[1] - neg[2],
    ]


def collide_tile(f, kind, porous, want_post=True):
    inlet, turn, rate = cell_kinds(kind)
    s, d, big, off, e, g = moments(f)
    axis_sum = s[0] + s[1] + s[2]
    edge_sum = big[0] + big[1] + big[2]
    rho = f[0] + axis_sum + edge_sum
    eg = [e[a] + g[a] for a in range(3)]
    j = [d[a] + eg[a] for a in range(3)]
    inv = 1.0 / rho
    u = [j[a] * inv for a in range(3)]
    xx, yy, zz = j[0] * u[0], j[1] * u[1], j[2] * u[2]
    energy = xx + yy + zz
    e1 = rate(R_E, 1 / 126) * (edge_sum - f[0] - energy)
    r_eps = rate(R_EPS, 1.0)
    e2 = (r_eps * (1 / 252)) * (9.0 * f[0] - 7.0 * axis_sum - 2.0 * edge_sum + 5.5 * energy)
    r_nu = rate(R_NU, 1.0)
    yz_a, yz_e, yz_u = s[1] - s[2], big[0] - big[1], yy - zz
    x_a = 2.0 * s[0] - (s[1] + s[2])
    x_e = big[0] + big[1] - 2.0 * big[2]
    x_u = 2.0 * xx - (yy + zz)
    p1 = (r_nu * (1 / 18)) * (x_a + x_e - x_u)
    q1 = (r_eps * (1 / 36)) * (x_e - 2.0 * x_a + 0.5 * x_u)
    p2 = (r_nu * (1 / 6)) * (yz_a + yz_e - yz_u)
    q2 = (r_eps * (1 / 12)) * (yz_e - 2.0 * yz_a + 0.5 * yz_u)
    half_nu = r_nu * 0.5
    t = [half_nu * (off[0] - j[0] * u[1]), half_nu * (off[1] - j[0] * u[2]), half_nu * (off[2] - j[1] * u[2])]
    r_q, r_m = rate(R_Q, 1 / 12), rate(R_M, 1 / 4)
    q = [r_q * (eg[a] - 2.0 * d[a]) for a in range(3)]
    m = [r_m * (e[a] - g[a]) for a in range(3)]
    zero, sums = spread(e1, e2, p1 - 2.0 * q1, p1 + q1, p2 - 2.0 * q2, p2 + q2, t, q, m)
    diffs = odd_terms(q, m, None)
    gap0 = jnp.where(inlet, f[0] - IN_NO / 3, zero)
    gap = [None] * 19
    gap[0] = gap0
    post = [None] * 19
    share = 1.0 - porous
    half = 0.5 * share
    if want_post:
        post[0] = f[0] - share * gap0
    for n, (a, b) in enumerate(PAIRS):
        weight = (1 / 9 if n < 3 else 1 / 18)
        has_x = VEL[a][0] != 0
        in_s = weight * (IN_CX if has_x else IN_NO)
        in_d = weight * 0.15 if has_x else 0.0
        gs = jnp.where(inlet, s[n] - in_s, sums[n])
        gd = diffs[n] - turn * d[n]
        if has_x:
            gd = jnp.where(inlet, gd - in_d, gd)
        gap[a], gap[b] = gs + gd, gs - gd
        if want_post:
            post[a] = f[b] - half * gap[a]
            post[b] = f[a] - half * gap[b]
    return post, u, gap


def adjoint_tile(b, u, kind, porous):
    inlet, turn, rate = cell_kinds(kind)
    s, d, big, off, e, g = moments(b)
    axis_sum = s[0] + s[1] + s[2]
    edge_sum = big[0] + big[1] + big[2]
    eg = [e[a] + g[a] for a in range(3)]
    e1 = rate(R_E, 1 / 2394) * (8.0 * edge_sum - 11.0 * axis_sum - 30.0 * b[0])
    r_eps = rate(R_EPS, 1.0)
    e2 = (r_eps * (1 / 252)) * (12.0 * b[0] - 4.0 * axis_sum + edge_sum)
    r_nu = rate(R_NU, 1.0)
    yz_a, yz_e = s[1] - s[2], big[0] - big[1]
    x_a = 2.0 * s[0] - (s[1] + s[2])
    x_e = big[0] + big[1] - 2.0 * big[2]
    p1 = (r_nu * (1 / 18)) * (x_a + x_e)
    q1 = (r_eps * (1 / 36)) * (x_e - 2.0 * x_a)
    p2 = (r_nu * (1 / 6)) * (yz_a + yz_e)
    q2 = (r_eps * (1 / 12)) * (yz_e - 2.0 * yz_a)
    half_nu = r_nu * 0.5
    t = [half_nu * off[n] for n in range(3)]
    r_q, r_m = rate(R_Q, 1 / 20), rate(R_M, 1 / 4)
    q = [r_q * (eg[a] - 4.0 * d[a]) for a in range(3)]
    m = [r_m * (e[a] - g[a]) for a in range(3)]
    common = 38.0 * e1 - 11.0 * e2
    v = p1 - 0.5 * q1
    w = p2 - 0.5 * q2
    k = [common + 2.0 * v, common - v + w, common - v - w]
    k2 = [k[a] + k[a] for a in range(3)]
    gx = k2[0] * u[0] + t[0] * u[1] + t[1] * u[2]
    gy = k2[1] * u[1] + t[0] * u[0] + t[2] * u[2]
    gz = k2[2] * u[2] + t[1] * u[0] + t[2] * u[1]
    quad = 0.5 * (gx * u[0] + gy * u[1] + gz * u[2])
    by_rho = 6.0 * e2 - 22.0 * e1 - quad
    by_j = [gx - (2 / 3) * q[0], gy - (2 / 3) * q[1], gz - (2 / 3) * q[2]]
    zero, sums = spread(e1, e2, p1 - 2.0 * q1, p1 + q1, p2 - 2.0 * q2, p2 + q2, t, q, m)
    diffs = odd_terms(q, m, by_j)
    zero = zero - 0.5 * by_rho
    share = 1.0 - porous
    half = 0.5 * share
    out = [None] * 19
    out[0] = b[0] - share * jnp.where(inlet, b[0], zero)
    for n, (a, c) in enumerate(PAIRS):
        gs = jnp.where(inlet, s[n], sums[n] - by_rho)
        gd = diffs[n] - turn * d[n]
        out[a] = b[c] - half * (gs + gd)
        out[c] = b[a] - half * (gs - gd)
    return out


def dot_gap(b, gap):
    total = (b[1] * gap[1] + b[2] * gap[2]) + (b[3] * gap[3] + b[4] * gap[4])
    for i in range(5, 19):
        total = total + b[i] * gap[i]
    return b[0] * gap[0] + 0.5 * total


def iota(axis):
    return lax.broadcasted_iota(jnp.int32, (8, LANES), axis)


def pull(load, lane, sense, column, ring, split=False):
    z = lane & (NZ - 1)
    lower = lane < 64

    def shifted(plane, off_x, amount):
        if split:
            high, low = load(plane, 2, off_x), load(plane, 3, off_x)
            if amount == 0:
                return jnp.where(lower, high, low)
            if amount > 0:
                mixed = jnp.where(lane < 64 - amount, high, jnp.where(lane < LANES - amount, low, load(plane, 1, off_x)))
            else:
                mixed = jnp.where(lane < -amount, load(plane, 0, off_x), jnp.where(lane < 64 - amount, high, low))
            return pltpu.roll(mixed, amount % LANES, 1)
        here = load(plane, column, off_x)
        if amount == 0:
            return here
        there = load(plane, (column + (-1 if amount > 0 else 1)) % ring, off_x)
        if amount > 0:
            mixed = jnp.where(lane >= LANES - amount, there, here)
        else:
            mixed = jnp.where(lane < -amount, there, here)
        return pltpu.roll(mixed, amount % LANES, 1)

    arrived = []
    for i, (cx, cy, cz) in enumerate(VEL):
        value = shifted(i, -sense * cx, sense * (NZ * cy + cz))
        if cz != 0:
            edge = 0 if sense * cz == 1 else NZ - 1
            value = jnp.where(z == edge, shifted(OPP[i], 0, 0), value)
        arrived.append(value)
    return arrived


def counts(c):
    return (5 - c, 3 + c), (5 + c, 3 - c)


def first_kernel(
    snap_hbm, flag_hbm, por_hbm, adj_hbm, post_ref, adj_ref, u_ref, gap_ref, xp_ref, out_ref, in_ref, dg_ref,
    snap_ref, flag_ref, por_ref, sems,
):
    core = lax.rem(lax.axis_index("gy"), 2)
    rows = snap_ref.shape[1]
    lane, row = iota(1), iota(0)
    copies = [(flag_hbm, flag_ref), (por_hbm, por_ref)]
    copies += [(snap_hbm.at[:, 8 * g : 8 * g + 8], snap_ref.at[:, 8 * g : 8 * g + 8]) for g in range(rows // 8)]
    copies += [(adj_hbm, adj_ref)]
    copies = [pltpu.make_async_copy(src, dst, sems.at[n]) for n, (src, dst) in enumerate(copies)]
    for copy in copies:
        copy.start()
    copies[0].wait()
    copies[1].wait()
    for g in range(rows // 8):
        copies[2 + g].wait()
        at = slice(8 * g, 8 * g + 8)
        for c in range(2):
            lanes = slice(c * LANES, (c + 1) * LANES)
            kind, porous = flag_ref[at, lanes].astype(F32), por_ref[at, lanes]
            post, u, gap = collide_tile([snap_ref[i, at, lanes] for i in range(19)], kind, porous)
            for i, value in enumerate(post + [porous, kind]):
                post_ref[i, at, lanes] = value
            for i in range(19):
                gap_ref[i, at, lanes] = gap[i]
            for a in range(3):
                u_ref[a, at, lanes] = u[a]
    copies[-1].wait()

    def plane(i, at, lanes):
        return post_ref[i, at, lanes]

    def low_spare(i, at, lanes, axis, where, unit, roll):
        value, first = plane(i, at, lanes), WALL[axis]
        extras = [(post_ref, 0, 4, 5), (post_ref, 1, 4, 6), (adj_ref, 2, 2, 7)] if i == 19 else [(adj_ref, 3, 2, 5)]
        for ref, n, layer, slot in extras:
            moved = roll(ref[first + n, at, lanes], unit * (slot - layer))
            value = jnp.where(where >= unit * slot, moved, value)
        return value

    def high_spare(i, at, lanes, axis, where, unit, roll):
        value, first = plane(i, at, lanes), WALL[axis]
        extras = [(post_ref, 2, 3, 2), (adj_ref, 1, 5, 1), (adj_ref, 0, 5, 0)] if i == 19 else [(post_ref, 3, 3, 2)]
        for ref, n, layer, slot in extras:
            moved = roll(ref[first + n, at, lanes], (unit * (slot - layer)) % (unit * 8))
            value = jnp.where(where < unit * (slot + 1), moved, value)
        return value

    def roll_rows(value, amount):
        return pltpu.roll(value, amount, 0)

    def roll_lanes(value, amount):
        return pltpu.roll(value, amount, 1)

    low_rows, high_rows = slice(0, 8), slice(rows - 8, rows)
    for c in range(2):
        lanes = slice(c * LANES, (c + 1) * LANES)
        for i in range(21):
            low, high = plane(i, low_rows, lanes), plane(i, high_rows, lanes)
            if i < 19:
                (n_low, _), (_, m_high) = counts(VEL[i][0])
                low = jnp.where(row < n_low, low, pltpu.roll(adj_ref[i, low_rows, lanes], n_low, 0))
                high = jnp.where(row >= m_high, high, pltpu.roll(adj_ref[i, high_rows, lanes], m_high, 0))
            else:
                low = low_spare(i, low_rows, lanes, 0, row, 1, roll_rows)
                high = high_spare(i, high_rows, lanes, 0, row, 1, roll_rows)
            xp_ref[0, i, :, lanes] = low
            xp_ref[1, i, :, lanes] = high

            @pl.when(core == c)
            def _():
                dg_ref[0, i] = low
                dg_ref[1, i] = high

    def pack_low(dst):
        for i in range(21):
            for g in range(rows // 8):
                at = slice(8 * g, 8 * g + 8)
                value = plane(i, at, slice(0, LANES))
                if i < 19:
                    (n, _), _ = counts(VEL[i][1])
                    value = jnp.where(lane < NZ * n, value, pltpu.roll(adj_ref[i, at, slice(0, LANES)], NZ * n, 1))
                else:
                    value = low_spare(i, at, slice(0, LANES), 1, lane, NZ, roll_lanes)
                dst[i, at, :] = value

    def pack_high(dst):
        for i in range(21):
            for g in range(rows // 8):
                at = slice(8 * g, 8 * g + 8)
                value = plane(i, at, slice(LANES, 2 * LANES))
                if i < 19:
                    _, (_, m) = counts(VEL[i][1])
                    value = jnp.where(lane >= NZ * m, value, pltpu.roll(adj_ref[i, at, slice(LANES, 2 * LANES)], NZ * m, 1))
                else:
                    value = high_spare(i, at, slice(LANES, 2 * LANES), 1, lane, NZ, roll_lanes)
                dst[i, at, :] = value

    @pl.when(core == 0)
    def _():
        pack_low(out_ref)
        pack_high(in_ref)

    @pl.when(core == 1)
    def _():
        pack_low(in_ref)
        pack_high(out_ref)


def second_kernel(
    post_in, adj_in, u0_ref, gap0_ref, xr, out_in, in_in, dg_in, xin, res_hbm, sens_hbm,
    p0, p1, p2, pe, u1, u2, u3, g1, g2, g3, a4, a3, a2, a1, s1, s2, s3, res_ref, sens_ref, sems,
):
    first_core = lax.rem(lax.axis_index("gy"), 2) == 0
    rows = post_in.shape[1]
    groups = rows // 8
    lane = iota(1)
    lower = lane < 64
    roll_lanes = lambda value, amount: pltpu.roll(value, amount % LANES, 1)
    roll_rows = lambda value, amount: pltpu.roll(value, amount % 8, 0)

    def beside(i, at):
        out, inside = out_in[i, at], in_in[i, at]
        return jnp.where(first_core, inside, out), jnp.where(first_core, out, inside)

    def corner(side, i):
        out, near, far = dg_in[side, i], xin[side, i, :, 0:LANES], xin[side, i, :, LANES:]
        return jnp.where(first_core, near, out), jnp.where(first_core, out, far)

    top, bottom = slice(8 + rows, 16 + rows), slice(0, 8)
    for g in range(groups):
        at, to = slice(8 * g, 8 * g + 8), slice(8 + 8 * g, 16 + 8 * g)
        spare = {}
        for i in (19, 20) + tuple(range(19)):
            high, low = beside(i, at)
            if i >= 19:
                spare[i] = (high, low)
                pe[i - 19, to] = jnp.where(lower, high, low)
            p0[i, 0, to] = post_in[i, at, 0:LANES]
            p0[i, 1, to] = post_in[i, at, LANES:]
            n = i - WALL[1]
            p0[i, 2, to] = jnp.where(lower, high, roll_lanes(spare[19][0], -NZ * (1 + n))) if n in (0, 1) else high
            p0[i, 3, to] = jnp.where(lower, roll_lanes(spare[17 + n][1], NZ), low) if n in (2, 3) else low
            if i < 19:
                (n_low, _), (_, m_high) = counts(VEL[i][1])
                high, low = roll_lanes(high, -NZ * n_low), roll_lanes(low, -NZ * m_high)
                if n in (0, 1):
                    low = jnp.where(lane >= 96, low, roll_lanes(spare[19][1], NZ * (5 - n)))
                if n in (2, 3):
                    high = jnp.where(lane < 32, high, roll_lanes(spare[17 + n][0], -NZ * ((7, 5)[n - 2] - 2)))
                a4[i, 0, to] = adj_in[i, at, 0:LANES]
                a4[i, 1, to] = adj_in[i, at, LANES:]
                a4[i, 2, to] = jnp.where(lower, high, low)
    for side, to in ((0, top), (1, bottom)):
        for i in range(21):
            high, low = corner(side, i)
            tile = [xr[side, i, :, 0:LANES], xr[side, i, :, LANES:], high, low]
            edge = jnp.where(lower, high, low)
            for c in range(4):
                p0[i, c, to] = tile[c]
            if i >= 19:
                pe[i - 19, to] = edge
                continue
            (n_low, _), (_, m_high) = counts(VEL[i][0])
            for c, value in enumerate((tile[0], tile[1], edge)):
                a4[i, c, to] = roll_rows(value, -n_low if side == 0 else -m_high)
    moves = [(p0, 0, 19, 8 + rows + 5, 8 + rows + 4), (p0, 1, 19, 8 + rows + 6, 8 + rows + 4)]
    moves += [(a4, 2, 19, 8 + rows + 7, 8 + rows + 2), (a4, 3, 20, 8 + rows + 5, 8 + rows + 2)]
    moves += [(a4, 0, 19, 0, 5), (a4, 1, 19, 1, 5), (p0, 2, 19, 2, 3), (p0, 3, 20, 2, 3)]
    for dst, n, src, row, to in moves:
        for c in range(4):
            if dst is p0:
                dst[WALL[0] + n, c, to : to + 1] = p0[src, c, row : row + 1]
            elif c < 3:
                dst[WALL[0] + n, c, to : to + 1] = pe[src - 19, row : row + 1] if c == 2 else p0[src, c, row : row + 1]

    def kinds(c, cells, ring):
        if ring == 3 and c == 2:
            return pe[1, cells], pe[0, cells]
        return p0[20, c, cells], p0[19, c, cells]

    def forward(src, src_base, base, n_groups, src_ring, ring, post_dst, u_dst, gap_dst):
        def body(k, carry):
            def load(i, c, off):
                return src[i, c, pl.ds(8 * k + (base - src_base + off), 8)]

            at = pl.ds(pl.multiple_of(8 * k, 8), 8)
            cells = pl.ds(8 * k + (base + 8), 8)
            sides = []
            for c in range(ring):
                f = pull(load, lane, 1, c, src_ring, src_ring != ring and c == 2)
                post, u, gap = collide_tile(f, *kinds(c, cells, ring), post_dst is not None)
                if post_dst is not None:
                    for i in range(19):
                        post_dst[i, c, at] = post[i]
                if c < 2:
                    for i in range(19):
                        gap_dst[i, c, at] = gap[i]
                elif ring == 4:
                    sides.append(u)
                    if c == 2:
                        continue
                    u, c = [jnp.where(lower, a, b) for a, b in zip(*sides)], 2
                for a in range(3):
                    u_dst[a, c, at] = u[a]
            return carry

        lax.fori_loop(0, n_groups, body, 0)

    forward(p0, -8, -5, groups + 2, 4, 4, p1, u1, g1)
    forward(p1, -5, -4, groups + 1, 4, 3, p2, u2, g2)
    forward(p2, -4, -3, groups + 1, 3, 3, None, u3, g3)

    def backward(src, src_base, base, dst, u_src, gap_src, f_base, s_dst):
        def body(k, carry):
            def load(i, c, off):
                return src[i, c, pl.ds(8 * k + (base - src_base + off), 8)]

            at = pl.ds(pl.multiple_of(8 * k, 8), 8)
            cells = pl.ds(8 * k + (base + 8), 8)
            old = pl.ds(8 * k + (base - f_base), 8)
            for c in range(3):
                b = pull(load, lane, -1, c, 3)
                if c < 2:
                    s_dst[c, at] = dot_gap(b, [gap_src[i, c, old] for i in range(19)])
                a = adjoint_tile(b, [u_src[n, c, old] for n in range(3)], *kinds(c, cells, 3))
                for i in range(19):
                    dst[i, c, at] = a[i]
            return carry

        lax.fori_loop(0, groups + 1, body, 0)

    backward(a4, -8, -3, a3, u3, g3, -3, s3)
    backward(a3, -3, -2, a2, u2, g2, -4, s2)
    backward(a2, -2, -1, a1, u1, g1, -5, s1)

    def results(k):
        at = pl.ds(pl.multiple_of(8 * k, 8), 8)
        return pltpu.make_async_copy(res_ref.at[:, at], res_hbm.at[:, at], sems.at[k])

    def last(k, carry):
        at = pl.ds(pl.multiple_of(8 * k, 8), 8)

        def load(i, c, off):
            return a1[i, c, pl.ds(8 * k + (1 + off), 8)]

        for c in range(2):
            lanes = slice(c * LANES, (c + 1) * LANES)
            b = pull(load, lane, -1, c, 3)
            total = dot_gap(b, [gap0_ref[i, at, lanes] for i in range(19)])
            later = s3[c, pl.ds(8 * k + 3, 8)] + s2[c, pl.ds(8 * k + 2, 8)] + s1[c, pl.ds(8 * k + 1, 8)]
            sens_ref[at, lanes] = total + later
            a = adjoint_tile(b, [u0_ref[n, at, lanes] for n in range(3)], post_in[20, at, lanes], post_in[19, at, lanes])
            for i in range(19):
                res_ref[i, at, lanes] = a[i]
        results(k).start()
        return carry

    lax.fori_loop(0, groups, last, 0)
    sens_copy = pltpu.make_async_copy(sens_ref, sens_hbm, sems.at[groups])
    sens_copy.start()
    for k in range(groups):
        results(k).wait()
    sens_copy.wait()


VMEM = pl.BlockSpec(memory_space=pltpu.VMEM)
HBM = pl.BlockSpec(memory_space=pltpu.HBM)


def exchange(xp, out, inside, dg):
    nx, ny = lax.axis_size("gx"), lax.axis_size("gy")
    same = [(i, i ^ 1) for i in range(ny)]
    other = [(i, (i + 1) % ny if i % 2 else (i - 1) % ny) for i in range(ny)]

    def along(value, axes, pairs_of):
        if nx == 2:
            return lax.ppermute(value, axes, pairs_of(1))
        return jnp.stack([lax.ppermute(value[0], axes, pairs_of(-1)), lax.ppermute(value[1], axes, pairs_of(1))])

    xr = along(xp, "gx", lambda step: [(i, (i + step) % nx) for i in range(nx)])
    out_r = lax.ppermute(out, "gy", other)
    dg_r = along(
        dg, ("gx", "gy"), lambda step: [(i * ny + j, ((i + step) % nx) * ny + k) for i in range(nx) for j, k in other]
    )
    in_r = lax.ppermute(inside, "gy", same)
    xr, out_r, dg_r, in_r = lax.optimization_barrier((xr, out_r, dg_r, in_r))
    xin = lax.ppermute(xr, "gy", same)
    return xr, out_r, in_r, dg_r, xin


def per_device(snapshot, flags, porosity, adjoint_end):
    _, rows, lanes = snapshot.shape
    assert lanes == 2 * LANES and rows % 8 == 0

    def array(*shape):
        return jax.ShapeDtypeStruct(shape, F32)

    def scratch(*shape):
        return pltpu.VMEM(shape, F32)

    groups = rows // 8
    post, adj, u0, gap0, xp, out, inside, dg = pl.pallas_call(
        first_kernel,
        out_shape=(
            array(21, rows, lanes), array(19, rows, lanes), array(3, rows, lanes), array(19, rows, lanes),
            array(2, 21, 8, lanes), array(21, rows, LANES), array(21, rows, LANES), array(2, 21, 8, LANES),
        ),
        in_specs=[HBM] * 4,
        out_specs=(VMEM,) * 8,
        scratch_shapes=[
            scratch(19, rows, lanes), pltpu.VMEM((rows, lanes), jnp.int32), scratch(rows, lanes),
            pltpu.SemaphoreType.DMA((groups + 3,)),
        ],
        compiler_params=pltpu.CompilerParams(vmem_limit_bytes=12 << 20),
        name="collide_and_pack",
    )(*[pltpu.with_memory_space_constraint(v, pltpu.HBM) for v in (snapshot, flags, porosity, adjoint_end)])
    received = exchange(xp, out, inside, dg)
    tall, mid = rows + 24, rows + 16
    return pl.pallas_call(
        second_kernel,
        out_shape=(array(19, rows, lanes), array(rows, lanes)),
        in_specs=[VMEM] * 9,
        out_specs=(HBM, HBM),
        scratch_shapes=[
            scratch(21, 4, tall, LANES), scratch(19, 4, tall, LANES), scratch(19, 3, tall, LANES), scratch(2, tall, LANES),
            scratch(3, 3, mid, LANES), scratch(3, 3, mid, LANES), scratch(3, 3, mid, LANES),
            scratch(19, 2, mid, LANES), scratch(19, 2, mid, LANES), scratch(19, 2, mid, LANES),
            scratch(19, 3, mid, LANES), scratch(19, 3, mid, LANES), scratch(19, 3, mid, LANES), scratch(19, 3, mid, LANES),
            scratch(2, mid, LANES), scratch(2, mid, LANES), scratch(2, mid, LANES),
            scratch(19, rows, lanes), scratch(rows, lanes), pltpu.SemaphoreType.DMA((groups + 1,)),
        ],
        compiler_params=pltpu.CompilerParams(vmem_limit_bytes=28 << 20),
        name="window",
    )(post, adj, u0, gap0, *received)


def solution(mesh):
    placed = (P(None, "gx", "gy"), P("gx", "gy"), P("gx", "gy"), P(None, "gx", "gy"))
    return jax.shard_map(
        per_device,
        mesh=mesh,
        in_specs=placed,
        out_specs=(P(None, "gx", "gy"), P("gx", "gy")),
        check_vma=False,
    )
```

```python
import jax
import jax.numpy as jnp
from jax import lax
from jax.experimental import pallas as pl
from jax.experimental.pallas import tpu as pltpu
from jax.sharding import PartitionSpec as P

NZ = 16
LANES = 128
F32 = jnp.float32


def velocity_list():
    found = [(0, 0, 0)]
    for axis in range(3):
        for sense in (1, -1):
            vector = [0, 0, 0]
            vector[axis] = sense
            found.append(tuple(vector))
    for a, b in ((0, 1), (0, 2), (1, 2)):
        for sense_a in (1, -1):
            for sense_b in (1, -1):
                vector = [0, 0, 0]
                vector[a], vector[b] = sense_a, sense_b
                found.append(tuple(vector))
    return found


VEL = velocity_list()
OPP = [VEL.index(tuple(-v for v in c)) for c in VEL]
PAIRS = [(1, 2), (3, 4), (5, 6), (7, 10), (8, 9), (11, 14), (12, 13), (15, 18), (16, 17)]
R_E, R_EPS, R_Q, R_NU, R_PI, R_M = 1.19, 1.4, 1.2, 1.0 / 0.6, 1.4, 1.98
WALL = (11, 15)
IN_CX, IN_NO = 1 + 0.01125 - 0.00375, 1 - 0.00375


def cell_kinds(kind):
    fluid, outlet, inlet, wall = kind == 0.0, kind == 3.0, kind == 2.0, kind == 1.0

    def rate(value, scale):
        return jnp.where(fluid, value * scale, jnp.where(outlet, scale, 0.0)).astype(F32)

    turn = jnp.where(wall, 0.0, jnp.where(inlet, 1.0, 2.0)).astype(F32)
    return inlet, turn, rate


def moments(f):
    s = [f[a] + f[b] for a, b in PAIRS]
    d = [f[a] - f[b] for a, b in PAIRS]
    big_s = [s[3] + s[4], s[5] + s[6], s[7] + s[8]]
    off = [s[3] - s[4], s[5] - s[6], s[7] - s[8]]
    ex, gy = d[3] + d[4], d[3] - d[4]
    gx, ez = d[5] + d[6], d[5] - d[6]
    ey, gz = d[7] + d[8], d[7] - d[8]
    return s, d, big_s, off, (ex, ey, ez), (gx, gy, gz)


def spread(e1, e2, a1, b1, a2, b2, t, q, m):
    zero = 12.0 * e2 - 30.0 * e1
    axis = -22.0 * e1 - 8.0 * e2
    edge = 16.0 * e1 + 2.0 * e2
    xy, xz, yz = edge + b1 + b2, edge + b1 - b2, edge - 2.0 * b1
    sums = [
        axis + 2.0 * a1, axis - a1 + a2, axis - a1 - a2,
        xy + t[0], xy - t[0], xz + t[1], xz - t[1], yz + t[2], yz - t[2],
    ]
    return zero, sums


def odd_terms(q, m, j):
    if j is None:
        along = [-4.0 * q[a] for a in range(3)]
        pos = [q[a] + m[a] for a in range(3)]
        neg = [q[a] - m[a] for a in range(3)]
    else:
        along = [-4.0 * q[a] - j[a] for a in range(3)]
        base = [q[a] - j[a] for a in range(3)]
        pos = [base[a] + m[a] for a in range(3)]
        neg = [base[a] - m[a] for a in range(3)]
    return along + [
        pos[0] + neg[1], pos[0] - neg[1], neg[0] + pos[2], neg[0] - pos[2], pos[1] + neg[2], pos[1] - neg[2],
    ]


def collide_tile(f, kind, porous, want_post=True):
    inlet, turn, rate = cell_kinds(kind)
    s, d, big, off, e, g = moments(f)
    axis_sum = s[0] + s[1] + s[2]
    edge_sum = big[0] + big[1] + big[2]
    rho = f[0] + axis_sum + edge_sum
    eg = [e[a] + g[a] for a in range(3)]
    j = [d[a] + eg[a] for a in range(3)]
    inv = 1.0 / rho
    u = [j[a] * inv for a in range(3)]
    xx, yy, zz = j[0] * u[0], j[1] * u[1], j[2] * u[2]
    energy = xx + yy + zz
    e1 = rate(R_E, 1 / 126) * (edge_sum - f[0] - energy)
    r_eps = rate(R_EPS, 1.0)
    e2 = (r_eps * (1 / 252)) * (9.0 * f[0] - 7.0 * axis_sum - 2.0 * edge_sum + 5.5 * energy)
    r_nu = rate(R_NU, 1.0)
    yz_a, yz_e, yz_u = s[1] - s[2], big[0] - big[1], yy - zz
    x_a = 2.0 * s[0] - (s[1] + s[2])
    x_e = big[0] + big[1] - 2.0 * big[2]
    x_u = 2.0 * xx - (yy + zz)
    p1 = (r_nu * (1 / 18)) * (x_a + x_e - x_u)
    q1 = (r_eps * (1 / 36)) * (x_e - 2.0 * x_a + 0.5 * x_u)
    p2 = (r_nu * (1 / 6)) * (yz_a + yz_e - yz_u)
    q2 = (r_eps * (1 / 12)) * (yz_e - 2.0 * yz_a + 0.5 * yz_u)
    half_nu = r_nu * 0.5
    t = [half_nu * (off[0] - j[0] * u[1]), half_nu * (off[1] - j[0] * u[2]), half_nu * (off[2] - j[1] * u[2])]
    r_q, r_m = rate(R_Q, 1 / 12), rate(R_M, 1 / 4)
    q = [r_q * (eg[a] - 2.0 * d[a]) for a in range(3)]
    m = [r_m * (e[a] - g[a]) for a in range(3)]
    zero, sums = spread(e1, e2, p1 - 2.0 * q1, p1 + q1, p2 - 2.0 * q2, p2 + q2, t, q, m)
    diffs = odd_terms(q, m, None)
    gap0 = jnp.where(inlet, f[0] - IN_NO / 3, zero)
    gap = [None] * 19
    gap[0] = gap0
    post = [None] * 19
    share = 1.0 - porous
    half = 0.5 * share
    if want_post:
        post[0] = f[0] - share * gap0
    for n, (a, b) in enumerate(PAIRS):
        weight = (1 / 9 if n < 3 else 1 / 18)
        has_x = VEL[a][0] != 0
        in_s = weight * (IN_CX if has_x else IN_NO)
        in_d = weight * 0.15 if has_x else 0.0
        gs = jnp.where(inlet, s[n] - in_s, sums[n])
        gd = diffs[n] - turn * d[n]
        if has_x:
            gd = jnp.where(inlet, gd - in_d, gd)
        gap[a], gap[b] = gs + gd, gs - gd
        if want_post:
            post[a] = f[b] - half * gap[a]
            post[b] = f[a] - half * gap[b]
    return post, u, gap


def adjoint_tile(b, u, kind, porous):
    inlet, turn, rate = cell_kinds(kind)
    s, d, big, off, e, g = moments(b)
    axis_sum = s[0] + s[1] + s[2]
    edge_sum = big[0] + big[1] + big[2]
    eg = [e[a] + g[a] for a in range(3)]
    e1 = rate(R_E, 1 / 2394) * (8.0 * edge_sum - 11.0 * axis_sum - 30.0 * b[0])
    r_eps = rate(R_EPS, 1.0)
    e2 = (r_eps * (1 / 252)) * (12.0 * b[0] - 4.0 * axis_sum + edge_sum)
    r_nu = rate(R_NU, 1.0)
    yz_a, yz_e = s[1] - s[2], big[0] - big[1]
    x_a = 2.0 * s[0] - (s[1] + s[2])
    x_e = big[0] + big[1] - 2.0 * big[2]
    p1 = (r_nu * (1 / 18)) * (x_a + x_e)
    q1 = (r_eps * (1 / 36)) * (x_e - 2.0 * x_a)
    p2 = (r_nu * (1 / 6)) * (yz_a + yz_e)
    q2 = (r_eps * (1 / 12)) * (yz_e - 2.0 * yz_a)
    half_nu = r_nu * 0.5
    t = [half_nu * off[n] for n in range(3)]
    r_q, r_m = rate(R_Q, 1 / 20), rate(R_M, 1 / 4)
    q = [r_q * (eg[a] - 4.0 * d[a]) for a in range(3)]
    m = [r_m * (e[a] - g[a]) for a in range(3)]
    common = 38.0 * e1 - 11.0 * e2
    v = p1 - 0.5 * q1
    w = p2 - 0.5 * q2
    k = [common + 2.0 * v, common - v + w, common - v - w]
    k2 = [k[a] + k[a] for a in range(3)]
    gx = k2[0] * u[0] + t[0] * u[1] + t[1] * u[2]
    gy = k2[1] * u[1] + t[0] * u[0] + t[2] * u[2]
    gz = k2[2] * u[2] + t[1] * u[0] + t[2] * u[1]
    quad = 0.5 * (gx * u[0] + gy * u[1] + gz * u[2])
    by_rho = 6.0 * e2 - 22.0 * e1 - quad
    by_j = [gx - (2 / 3) * q[0], gy - (2 / 3) * q[1], gz - (2 / 3) * q[2]]
    zero, sums = spread(e1, e2, p1 - 2.0 * q1, p1 + q1, p2 - 2.0 * q2, p2 + q2, t, q, m)
    diffs = odd_terms(q, m, by_j)
    zero = zero - 0.5 * by_rho
    share = 1.0 - porous
    half = 0.5 * share
    out = [None] * 19
    out[0] = b[0] - share * jnp.where(inlet, b[0], zero)
    for n, (a, c) in enumerate(PAIRS):
        gs = jnp.where(inlet, s[n], sums[n] - by_rho)
        gd = diffs[n] - turn * d[n]
        out[a] = b[c] - half * (gs + gd)
        out[c] = b[a] - half * (gs - gd)
    return out


def dot_gap(b, gap):
    total = (b[1] * gap[1] + b[2] * gap[2]) + (b[3] * gap[3] + b[4] * gap[4])
    for i in range(5, 19):
        total = total + b[i] * gap[i]
    return b[0] * gap[0] + 0.5 * total


def iota(axis):
    return lax.broadcasted_iota(jnp.int32, (8, LANES), axis)


def pull(load, lane, sense, column, ring, split=False):
    z = lane & (NZ - 1)
    lower = lane < 64

    def shifted(plane, off_x, amount):
        if split:
            high, low = load(plane, 2, off_x), load(plane, 3, off_x)
            if amount == 0:
                return jnp.where(lower, high, low)
            if amount > 0:
                mixed = jnp.where(lane < 64 - amount, high, jnp.where(lane < LANES - amount, low, load(plane, 1, off_x)))
            else:
                mixed = jnp.where(lane < -amount, load(plane, 0, off_x), jnp.where(lane < 64 - amount, high, low))
            return pltpu.roll(mixed, amount % LANES, 1)
        here = load(plane, column, off_x)
        if amount == 0:
            return here
        there = load(plane, (column + (-1 if amount > 0 else 1)) % ring, off_x)
        if amount > 0:
            mixed = jnp.where(lane >= LANES - amount, there, here)
        else:
            mixed = jnp.where(lane < -amount, there, here)
        return pltpu.roll(mixed, amount % LANES, 1)

    arrived = []
    for i, (cx, cy, cz) in enumerate(VEL):
        value = shifted(i, -sense * cx, sense * (NZ * cy + cz))
        if cz != 0:
            edge = 0 if sense * cz == 1 else NZ - 1
            value = jnp.where(z == edge, shifted(OPP[i], 0, 0), value)
        arrived.append(value)
    return arrived


def counts(c):
    return (5 - c, 3 + c), (5 + c, 3 - c)


def fold_tables(low, lane):
    tables = {}
    for c in (-1, 0, 1):
        cut = jnp.where(low, NZ * (5 - c), NZ * (3 - c))
        tables[c] = cut, jnp.where(low, lane - cut, cut - 1 - lane) < 0
    return tables


def wall_layers(low):
    where = jnp.where
    return [
        (0, (where(low, 4, 5), where(low, 5, 0))), (1, (where(low, 4, 5), where(low, 6, 1))),
        (2, (where(low, 2, 3), where(low, 7, 2))), (3, (where(low, 2, 3), where(low, 5, 2))),
    ]


def first_kernel(
    snap_hbm, flag_hbm, por_hbm, adj_hbm, post_ref, adj_ref, u_ref, gap_ref, xp_ref, out_ref, in_ref, dg_ref,
    snap_ref, flag_ref, por_ref, sems,
):
    core = lax.rem(lax.axis_index("gy"), 2)
    rows = snap_ref.shape[1]
    lane, row = iota(1), iota(0)
    copies = [(flag_hbm, flag_ref), (por_hbm, por_ref)]
    copies += [(snap_hbm.at[:, 8 * g : 8 * g + 8], snap_ref.at[:, 8 * g : 8 * g + 8]) for g in range(rows // 8)]
    copies += [(adj_hbm, adj_ref)]
    copies = [pltpu.make_async_copy(src, dst, sems.at[n]) for n, (src, dst) in enumerate(copies)]
    for copy in copies:
        copy.start()
    copies[0].wait()
    copies[1].wait()
    for g in range(rows // 8):
        copies[2 + g].wait()
        at = slice(8 * g, 8 * g + 8)
        for c in range(2):
            lanes = slice(c * LANES, (c + 1) * LANES)
            kind, porous = flag_ref[at, lanes].astype(F32), por_ref[at, lanes]
            post, u, gap = collide_tile([snap_ref[i, at, lanes] for i in range(19)], kind, porous)
            for i, value in enumerate(post + [porous, kind]):
                post_ref[i, at, lanes] = value
            for i in range(19):
                gap_ref[i, at, lanes] = gap[i]
            for a in range(3):
                u_ref[a, at, lanes] = u[a]
    copies[-1].wait()

    def plane(i, at, lanes):
        return post_ref[i, at, lanes]

    def low_spare(i, at, lanes, axis, where, unit, roll):
        value, first = plane(i, at, lanes), WALL[axis]
        extras = [(post_ref, 0, 4, 5), (post_ref, 1, 4, 6), (adj_ref, 2, 2, 7)] if i == 19 else [(adj_ref, 3, 2, 5)]
        for ref, n, layer, slot in extras:
            moved = roll(ref[first + n, at, lanes], unit * (slot - layer))
            value = jnp.where(where >= unit * slot, moved, value)
        return value

    def high_spare(i, at, lanes, axis, where, unit, roll):
        value, first = plane(i, at, lanes), WALL[axis]
        extras = [(post_ref, 2, 3, 2), (adj_ref, 1, 5, 1), (adj_ref, 0, 5, 0)] if i == 19 else [(post_ref, 3, 3, 2)]
        for ref, n, layer, slot in extras:
            moved = roll(ref[first + n, at, lanes], (unit * (slot - layer)) % (unit * 8))
            value = jnp.where(where < unit * (slot + 1), moved, value)
        return value

    def roll_rows(value, amount):
        return pltpu.roll(value, amount, 0)

    def roll_lanes(value, amount):
        return pltpu.roll(value, amount, 1)

    low_rows, high_rows = slice(0, 8), slice(rows - 8, rows)
    spare_rows, walls = [None] * 5, []
    folds = fold_tables(core == 0, lane)
    for i in range(21):
        lows, highs = [], []
        for c in range(2):
            lanes = slice(c * LANES, (c + 1) * LANES)
            if i < 19:
                (n_low, _), (_, m_high) = counts(VEL[i][0])
                low, high = plane(i, low_rows, lanes), plane(i, high_rows, lanes)
                low = jnp.where(row < n_low, low, pltpu.roll(adj_ref[i, low_rows, lanes], n_low, 0))
                high = jnp.where(row >= m_high, high, pltpu.roll(adj_ref[i, high_rows, lanes], m_high, 0))
            else:
                low = low_spare(i, low_rows, lanes, 0, row, 1, roll_rows)
                high = high_spare(i, high_rows, lanes, 0, row, 1, roll_rows)
            xp_ref[0, i, :, lanes] = low
            xp_ref[1, i, :, lanes] = high
            lows.append(low)
            highs.append(high)
        low, high = jnp.where(core == 0, *lows), jnp.where(core == 0, *highs)
        if len(dg_ref.shape) == 4:
            dg_ref[0, i], dg_ref[1, i] = low, high
        elif i >= 19:
            for n, (layer, slot) in wall_layers(core == 0):
                if (n == 3) == (i == 20):
                    kept = [pltpu.roll(t, (NZ * (slot - layer)) % LANES, 1) for t in walls[n]]
                    low, high = [jnp.where(lane // NZ == slot, k, t) for k, t in zip(kept, (low, high))]
            dg_ref[i], dg_ref[i + 2] = low, high
        else:
            if i >= WALL[1]:
                walls.append((low, high))
            cut, collided = folds[VEL[i][1]]
            own = jnp.where(row < n_low, low, high)
            other = jnp.where(row < n_low - 2, high, low)
            dg_ref[i] = jnp.where(collided, own, pltpu.roll(other, cut, 1))
            slot = 2 * (i % 4)
            moved = pltpu.roll(high, (slot - n_low + 2) % 8, 0)
            spare_rows[i // 4] = moved if slot == 0 else jnp.where(row < slot, spare_rows[i // 4], moved)
    if len(dg_ref.shape) == 3:
        for n in range(5):
            dg_ref[23 + n] = spare_rows[n]

    def pack_low(dst):
        for i in range(21):
            for g in range(rows // 8):
                at = slice(8 * g, 8 * g + 8)
                value = plane(i, at, slice(0, LANES))
                if i < 19:
                    (n, _), _ = counts(VEL[i][1])
                    value = jnp.where(lane < NZ * n, value, pltpu.roll(adj_ref[i, at, slice(0, LANES)], NZ * n, 1))
                else:
                    value = low_spare(i, at, slice(0, LANES), 1, lane, NZ, roll_lanes)
                dst[i, at, :] = value

    def pack_high(dst):
        for i in range(21):
            for g in range(rows // 8):
                at = slice(8 * g, 8 * g + 8)
                value = plane(i, at, slice(LANES, 2 * LANES))
                if i < 19:
                    _, (_, m) = counts(VEL[i][1])
                    value = jnp.where(lane >= NZ * m, value, pltpu.roll(adj_ref[i, at, slice(LANES, 2 * LANES)], NZ * m, 1))
                else:
                    value = high_spare(i, at, slice(LANES, 2 * LANES), 1, lane, NZ, roll_lanes)
                dst[i, at, :] = value

    @pl.when(core == 0)
    def _():
        pack_low(out_ref)
        pack_high(in_ref)

    @pl.when(core == 1)
    def _():
        pack_low(in_ref)
        pack_high(out_ref)


def second_kernel(
    post_in, adj_in, u0_ref, gap0_ref, xr, out_in, in_in, dg_in, xin, res_hbm, sens_hbm,
    p0, p1, p2, pe, u1, u2, u3, g1, g2, g3, a4, a3, a2, a1, s1, s2, s3, res_ref, sens_ref, sems,
):
    first_core = lax.rem(lax.axis_index("gy"), 2) == 0
    rows = post_in.shape[1]
    groups = rows // 8
    lane = iota(1)
    lower = lane < 64
    roll_lanes = lambda value, amount: pltpu.roll(value, amount % LANES, 1)
    roll_rows = lambda value, amount: pltpu.roll(value, amount % 8, 0)

    def beside(i, at):
        out, inside = out_in[i, at], in_in[i, at]
        return jnp.where(first_core, inside, out), jnp.where(first_core, out, inside)

    row = iota(0)
    folds = fold_tables(jnp.logical_not(first_core), lane)
    walls = wall_layers(jnp.logical_not(first_core))

    def outer_corner(side, i):
        if len(dg_in.shape) == 4:
            return dg_in[side, i]
        if i >= 19:
            return dg_in[i + 2 * side]
        tile, n = dg_in[i], 5 - VEL[i][0]
        other = pltpu.roll(tile, LANES - folds[VEL[i][1]][0], 1)
        if side == 0:
            tile = jnp.where(row < n, tile, other)
        else:
            spare = roll_rows(dg_in[23 + i // 4], n - 2 - 2 * (i % 4))
            tile = jnp.where(row >= n, tile, jnp.where(row >= n - 2, spare, other))
        if i >= WALL[1]:
            n, (layer, slot) = walls[i - WALL[1]]
            kept = pltpu.roll(dg_in[(20 if n == 3 else 19) + 2 * side], (NZ * (layer - slot)) % LANES, 1)
            tile = jnp.where(lane // NZ == layer, kept, tile)
        return tile

    def corner(side, i):
        out, near, far = outer_corner(side, i), xin[side, i, :, 0:LANES], xin[side, i, :, LANES:]
        return jnp.where(first_core, near, out), jnp.where(first_core, out, far)

    top, bottom = slice(8 + rows, 16 + rows), slice(0, 8)
    for g in range(groups):
        at, to = slice(8 * g, 8 * g + 8), slice(8 + 8 * g, 16 + 8 * g)
        spare = {}
        for i in (19, 20) + tuple(range(19)):
            high, low = beside(i, at)
            if i >= 19:
                spare[i] = (high, low)
                pe[i - 19, to] = jnp.where(lower, high, low)
            p0[i, 0, to] = post_in[i, at, 0:LANES]
            p0[i, 1, to] = post_in[i, at, LANES:]
            n = i - WALL[1]
            p0[i, 2, to] = jnp.where(lower, high, roll_lanes(spare[19][0], -NZ * (1 + n))) if n in (0, 1) else high
            p0[i, 3, to] = jnp.where(lower, roll_lanes(spare[17 + n][1], NZ), low) if n in (2, 3) else low
            if i < 19:
                (n_low, _), (_, m_high) = counts(VEL[i][1])
                high, low = roll_lanes(high, -NZ * n_low), roll_lanes(low, -NZ * m_high)
                if n in (0, 1):
                    low = jnp.where(lane >= 96, low, roll_lanes(spare[19][1], NZ * (5 - n)))
                if n in (2, 3):
                    high = jnp.where(lane < 32, high, roll_lanes(spare[17 + n][0], -NZ * ((7, 5)[n - 2] - 2)))
                a4[i, 0, to] = adj_in[i, at, 0:LANES]
                a4[i, 1, to] = adj_in[i, at, LANES:]
                a4[i, 2, to] = jnp.where(lower, high, low)
    for side, to in ((0, top), (1, bottom)):
        for i in range(21):
            high, low = corner(side, i)
            tile = [xr[side, i, :, 0:LANES], xr[side, i, :, LANES:], high, low]
            edge = jnp.where(lower, high, low)
            for c in range(4):
                p0[i, c, to] = tile[c]
            if i >= 19:
                pe[i - 19, to] = edge
                continue
            (n_low, _), (_, m_high) = counts(VEL[i][0])
            for c, value in enumerate((tile[0], tile[1], edge)):
                a4[i, c, to] = roll_rows(value, -n_low if side == 0 else -m_high)
    moves = [(p0, 0, 19, 8 + rows + 5, 8 + rows + 4), (p0, 1, 19, 8 + rows + 6, 8 + rows + 4)]
    moves += [(a4, 2, 19, 8 + rows + 7, 8 + rows + 2), (a4, 3, 20, 8 + rows + 5, 8 + rows + 2)]
    moves += [(a4, 0, 19, 0, 5), (a4, 1, 19, 1, 5), (p0, 2, 19, 2, 3), (p0, 3, 20, 2, 3)]
    for dst, n, src, row, to in moves:
        for c in range(4):
            if dst is p0:
                dst[WALL[0] + n, c, to : to + 1] = p0[src, c, row : row + 1]
            elif c < 3:
                dst[WALL[0] + n, c, to : to + 1] = pe[src - 19, row : row + 1] if c == 2 else p0[src, c, row : row + 1]

    def kinds(c, cells, ring):
        if ring == 3 and c == 2:
            return pe[1, cells], pe[0, cells]
        return p0[20, c, cells], p0[19, c, cells]

    def forward(src, src_base, base, n_groups, src_ring, ring, post_dst, u_dst, gap_dst):
        def body(k, carry):
            def load(i, c, off):
                return src[i, c, pl.ds(8 * k + (base - src_base + off), 8)]

            at = pl.ds(pl.multiple_of(8 * k, 8), 8)
            cells = pl.ds(8 * k + (base + 8), 8)
            sides = []
            for c in range(ring):
                f = pull(load, lane, 1, c, src_ring, src_ring != ring and c == 2)
                post, u, gap = collide_tile(f, *kinds(c, cells, ring), post_dst is not None)
                if post_dst is not None:
                    for i in range(19):
                        post_dst[i, c, at] = post[i]
                if c < 2:
                    for i in range(19):
                        gap_dst[i, c, at] = gap[i]
                elif ring == 4:
                    sides.append(u)
                    if c == 2:
                        continue
                    u, c = [jnp.where(lower, a, b) for a, b in zip(*sides)], 2
                for a in range(3):
                    u_dst[a, c, at] = u[a]
            return carry

        lax.fori_loop(0, n_groups, body, 0)

    forward(p0, -8, -5, groups + 2, 4, 4, p1, u1, g1)
    forward(p1, -5, -4, groups + 1, 4, 3, p2, u2, g2)
    forward(p2, -4, -3, groups + 1, 3, 3, None, u3, g3)

    def backward(src, src_base, base, dst, u_src, gap_src, f_base, s_dst):
        def body(k, carry):
            def load(i, c, off):
                return src[i, c, pl.ds(8 * k + (base - src_base + off), 8)]

            at = pl.ds(pl.multiple_of(8 * k, 8), 8)
            cells = pl.ds(8 * k + (base + 8), 8)
            old = pl.ds(8 * k + (base - f_base), 8)
            for c in range(3):
                b = pull(load, lane, -1, c, 3)
                if c < 2:
                    s_dst[c, at] = dot_gap(b, [gap_src[i, c, old] for i in range(19)])
                a = adjoint_tile(b, [u_src[n, c, old] for n in range(3)], *kinds(c, cells, 3))
                for i in range(19):
                    dst[i, c, at] = a[i]
            return carry

        lax.fori_loop(0, groups + 1, body, 0)

    backward(a4, -8, -3, a3, u3, g3, -3, s3)
    backward(a3, -3, -2, a2, u2, g2, -4, s2)
    backward(a2, -2, -1, a1, u1, g1, -5, s1)

    def results(k):
        at = pl.ds(pl.multiple_of(8 * k, 8), 8)
        return pltpu.make_async_copy(res_ref.at[:, at], res_hbm.at[:, at], sems.at[k])

    def last(k, carry):
        at = pl.ds(pl.multiple_of(8 * k, 8), 8)

        def load(i, c, off):
            return a1[i, c, pl.ds(8 * k + (1 + off), 8)]

        for c in range(2):
            lanes = slice(c * LANES, (c + 1) * LANES)
            b = pull(load, lane, -1, c, 3)
            total = dot_gap(b, [gap0_ref[i, at, lanes] for i in range(19)])
            later = s3[c, pl.ds(8 * k + 3, 8)] + s2[c, pl.ds(8 * k + 2, 8)] + s1[c, pl.ds(8 * k + 1, 8)]
            sens_ref[at, lanes] = total + later
            a = adjoint_tile(b, [u0_ref[n, at, lanes] for n in range(3)], post_in[20, at, lanes], post_in[19, at, lanes])
            for i in range(19):
                res_ref[i, at, lanes] = a[i]
        results(k).start()
        return carry

    lax.fori_loop(0, groups, last, 0)
    sens_copy = pltpu.make_async_copy(sens_ref, sens_hbm, sems.at[groups])
    sens_copy.start()
    for k in range(groups):
        results(k).wait()
    sens_copy.wait()


VMEM = pl.BlockSpec(memory_space=pltpu.VMEM)
HBM = pl.BlockSpec(memory_space=pltpu.HBM)


def exchange(xp, out, inside, dg):
    nx, ny = lax.axis_size("gx"), lax.axis_size("gy")
    same = [(i, i ^ 1) for i in range(ny)]
    other = [(i, (i + 1) % ny if i % 2 else (i - 1) % ny) for i in range(ny)]

    def along(value, axes, pairs_of):
        if nx == 2:
            return lax.ppermute(value, axes, pairs_of(1))
        return jnp.stack([lax.ppermute(value[0], axes, pairs_of(-1)), lax.ppermute(value[1], axes, pairs_of(1))])

    xr = along(xp, "gx", lambda step: [(i, (i + step) % nx) for i in range(nx)])
    out_r = lax.ppermute(out, "gy", other)
    dg_r = along(
        dg, ("gx", "gy"), lambda step: [(i * ny + j, ((i + step) % nx) * ny + k) for i in range(nx) for j, k in other]
    )
    in_r = lax.ppermute(inside, "gy", same)
    xr, out_r, dg_r, in_r = lax.optimization_barrier((xr, out_r, dg_r, in_r))
    xin = lax.ppermute(xr, "gy", same)
    return xr, out_r, in_r, dg_r, xin


def per_device(snapshot, flags, porosity, adjoint_end):
    _, rows, lanes = snapshot.shape
    assert lanes == 2 * LANES and rows % 8 == 0

    def array(*shape):
        return jax.ShapeDtypeStruct(shape, F32)

    def scratch(*shape):
        return pltpu.VMEM(shape, F32)

    groups = rows // 8
    post, adj, u0, gap0, xp, out, inside, dg = pl.pallas_call(
        first_kernel,
        out_shape=(
            array(21, rows, lanes), array(19, rows, lanes), array(3, rows, lanes), array(19, rows, lanes),
            array(2, 21, 8, lanes), array(21, rows, LANES), array(21, rows, LANES),
            array(*((28,) if lax.axis_size("gx") == 2 else (2, 21)), 8, LANES),
        ),
        in_specs=[HBM] * 4,
        out_specs=(VMEM,) * 8,
        scratch_shapes=[
            scratch(19, rows, lanes), pltpu.VMEM((rows, lanes), jnp.int32), scratch(rows, lanes),
            pltpu.SemaphoreType.DMA((groups + 3,)),
        ],
        compiler_params=pltpu.CompilerParams(vmem_limit_bytes=12 << 20),
        name="collide_and_pack",
    )(*[pltpu.with_memory_space_constraint(v, pltpu.HBM) for v in (snapshot, flags, porosity, adjoint_end)])
    received = exchange(xp, out, inside, dg)
    tall, mid = rows + 24, rows + 16
    return pl.pallas_call(
        second_kernel,
        out_shape=(array(19, rows, lanes), array(rows, lanes)),
        in_specs=[VMEM] * 9,
        out_specs=(HBM, HBM),
        scratch_shapes=[
            scratch(21, 4, tall, LANES), scratch(19, 4, tall, LANES), scratch(19, 3, tall, LANES), scratch(2, tall, LANES),
            scratch(3, 3, mid, LANES), scratch(3, 3, mid, LANES), scratch(3, 3, mid, LANES),
            scratch(19, 2, mid, LANES), scratch(19, 2, mid, LANES), scratch(19, 2, mid, LANES),
            scratch(19, 3, mid, LANES), scratch(19, 3, mid, LANES), scratch(19, 3, mid, LANES), scratch(19, 3, mid, LANES),
            scratch(2, mid, LANES), scratch(2, mid, LANES), scratch(2, mid, LANES),
            scratch(19, rows, lanes), scratch(rows, lanes), pltpu.SemaphoreType.DMA((groups + 1,)),
        ],
        compiler_params=pltpu.CompilerParams(vmem_limit_bytes=28 << 20),
        name="window",
    )(post, adj, u0, gap0, *received)


def solution(mesh):
    placed = (P(None, "gx", "gy"), P("gx", "gy"), P("gx", "gy"), P(None, "gx", "gy"))
    return jax.shard_map(
        per_device,
        mesh=mesh,
        in_specs=placed,
        out_specs=(P(None, "gx", "gy"), P("gx", "gy")),
        check_vma=False,
    )
```

```python
import jax
import jax.numpy as jnp
from jax import lax
from jax.experimental import pallas as pl
from jax.experimental.pallas import tpu as pltpu
from jax.sharding import PartitionSpec as P

NZ = 16
LANES = 128
F32 = jnp.float32


def velocity_list():
    found = [(0, 0, 0)]
    for axis in range(3):
        for sense in (1, -1):
            vector = [0, 0, 0]
            vector[axis] = sense
            found.append(tuple(vector))
    for a, b in ((0, 1), (0, 2), (1, 2)):
        for sense_a in (1, -1):
            for sense_b in (1, -1):
                vector = [0, 0, 0]
                vector[a], vector[b] = sense_a, sense_b
                found.append(tuple(vector))
    return found


VEL = velocity_list()
OPP = [VEL.index(tuple(-v for v in c)) for c in VEL]
PAIRS = [(1, 2), (3, 4), (5, 6), (7, 10), (8, 9), (11, 14), (12, 13), (15, 18), (16, 17)]
R_E, R_EPS, R_Q, R_NU, R_PI, R_M = 1.19, 1.4, 1.2, 1.0 / 0.6, 1.4, 1.98
WALL = (11, 15)
IN_CX, IN_NO = 1 + 0.01125 - 0.00375, 1 - 0.00375


def coefficients(kind, porous):
    half = 0.5 * (1.0 - porous)
    fluid, outlet, inlet, wall = kind == 0.0, kind == 3.0, kind == 2.0, kind == 1.0
    none = jnp.zeros_like(half)

    def rate(value, scale):
        return half * jnp.where(fluid, value * scale, jnp.where(outlet, scale, 0.0)).astype(F32)

    return [
        rate(R_E, 1 / 126), rate(R_EPS, 1 / 252), rate(R_NU, 1 / 18), rate(R_Q, 1 / 12), rate(R_M, 1 / 4),
        0.5 - jnp.where(inlet, half, none),
        jnp.where(wall, none, jnp.where(inlet, half, half + half)) - 0.5,
    ]


def moments(f):
    s = [f[a] + f[b] for a, b in PAIRS]
    d = [f[a] - f[b] for a, b in PAIRS]
    big_s = [s[3] + s[4], s[5] + s[6], s[7] + s[8]]
    off = [s[3] - s[4], s[5] - s[6], s[7] - s[8]]
    ex, gy = d[3] + d[4], d[3] - d[4]
    gx, ez = d[5] + d[6], d[5] - d[6]
    ey, gz = d[7] + d[8], d[7] - d[8]
    return s, d, big_s, off, (ex, ey, ez), (gx, gy, gz)


def even_terms(axis, edge, edge_yz, p1, q1, p2, q2, t):
    a1, b1, a2, b2 = p1 - 2.0 * q1, p1 + q1, p2 - 2.0 * q2, p2 + q2
    xy, xz, yz = edge + b1 + b2, edge + b1 - b2, edge_yz - 2.0 * b1
    return [
        axis[0] + 2.0 * a1, axis[1] - a1 + a2, axis[2] - a1 - a2,
        xy + t[0], xy - t[0], xz + t[1], xz - t[1], yz + t[2], yz - t[2],
    ]


def odd_terms(q, m, along, less):
    base = [q[a] if less[a] is None else q[a] - less[a] for a in range(3)]
    pos, neg = [base[a] + m[a] for a in range(3)], [base[a] - m[a] for a in range(3)]
    return along + [
        pos[0] + neg[1], pos[0] - neg[1], neg[0] + pos[2], neg[0] - pos[2], pos[1] + neg[2], pos[1] - neg[2],
    ]


def turned(f, s, d, zero, sums, diffs, keep, turn):
    out = [None] * 19
    out[0] = 2.0 * (keep * f[0] - zero)
    for n, (a, b) in enumerate(PAIRS):
        even, odd = keep * s[n] - sums[n], turn * d[n] - diffs[n]
        out[a], out[b] = even + odd, even - odd
    return out


def collide_tile(f, coefs):
    c_e, c_eps, c_nu, c_q, c_m, keep, turn = coefs
    s, d, big, off, e, g = moments(f)
    axis_sum = s[0] + s[1] + s[2]
    edge_sum = big[0] + big[1] + big[2]
    rho = f[0] + axis_sum + edge_sum
    eg = [e[a] + g[a] for a in range(3)]
    j = [d[a] + eg[a] for a in range(3)]
    inv = 1.0 / rho
    u = [j[a] * inv for a in range(3)]
    xx, yy, zz = j[0] * u[0], j[1] * u[1], j[2] * u[2]
    energy = xx + yy + zz
    e1 = c_e * (edge_sum - f[0] - energy)
    e2 = c_eps * (9.0 * f[0] - 7.0 * axis_sum - 2.0 * edge_sum + 5.5 * energy)
    yz_a, yz_e, yz_u = s[1] - s[2], big[0] - big[1], yy - zz
    x_a = 2.0 * s[0] - (s[1] + s[2])
    x_e = big[0] + big[1] - 2.0 * big[2]
    x_u = 2.0 * xx - (yy + zz)
    p1 = c_nu * (x_a + x_e - x_u)
    q1 = (7.0 * c_eps) * (x_e - 2.0 * x_a + 0.5 * x_u)
    p2 = (3.0 * c_nu) * (yz_a + yz_e - yz_u)
    q2 = (21.0 * c_eps) * (yz_e - 2.0 * yz_a + 0.5 * yz_u)
    c_off = 9.0 * c_nu
    t = [c_off * (off[0] - j[0] * u[1]), c_off * (off[1] - j[0] * u[2]), c_off * (off[2] - j[1] * u[2])]
    q = [c_q * (eg[a] - 2.0 * d[a]) for a in range(3)]
    m = [c_m * (e[a] - g[a]) for a in range(3)]
    inlet = 0.5 - keep
    axis, edge = -22.0 * e1 - 8.0 * e2, 16.0 * e1 + 2.0 * e2
    zero = 12.0 * e2 - 30.0 * e1 - inlet * (IN_NO / 3)
    axis_yz = axis - inlet * (IN_NO / 9)
    sums = even_terms(
        (axis - inlet * (IN_CX / 9), axis_yz, axis_yz), edge - inlet * (IN_CX / 18), edge - inlet * (IN_NO / 18), p1, q1, p2, q2, t
    )
    along = [-4.0 * q[0] - inlet * (0.15 / 9), -4.0 * q[1], -4.0 * q[2]]
    diffs = odd_terms(q, m, along, (inlet * (0.15 / 18), None, None))
    post = turned(f, s, d, zero, sums, diffs, keep, turn)
    return post, u, [f[OPP[i]] - post[i] for i in range(19)]


def adjoint_tile(b, u, coefs):
    c_e, c_eps, c_nu, c_q, c_m, keep, turn = coefs
    s, d, big, off, e, g = moments(b)
    axis_sum = s[0] + s[1] + s[2]
    edge_sum = big[0] + big[1] + big[2]
    eg = [e[a] + g[a] for a in range(3)]
    e1 = c_e * ((8 / 19) * edge_sum - (11 / 19) * axis_sum - (30 / 19) * b[0])
    e2 = c_eps * (12.0 * b[0] - 4.0 * axis_sum + edge_sum)
    yz_a, yz_e = s[1] - s[2], big[0] - big[1]
    x_a = 2.0 * s[0] - (s[1] + s[2])
    x_e = big[0] + big[1] - 2.0 * big[2]
    p1 = c_nu * (x_a + x_e)
    q1 = (7.0 * c_eps) * (x_e - 2.0 * x_a)
    p2 = (3.0 * c_nu) * (yz_a + yz_e)
    q2 = (21.0 * c_eps) * (yz_e - 2.0 * yz_a)
    c_off = 9.0 * c_nu
    t = [c_off * off[n] for n in range(3)]
    q = [c_q * (0.6 * eg[a] - 2.4 * d[a]) for a in range(3)]
    m = [c_m * (e[a] - g[a]) for a in range(3)]
    common = 76.0 * e1 - 22.0 * e2
    v, w = 2.0 * p1 - q1, 2.0 * p2 - q2
    less_v = common - v
    k = [common + 2.0 * v, less_v + w, less_v - w]
    gx = k[0] * u[0] + t[0] * u[1] + t[1] * u[2]
    gy = k[1] * u[1] + t[0] * u[0] + t[2] * u[2]
    gz = k[2] * u[2] + t[1] * u[0] + t[2] * u[1]
    by_rho = 6.0 * e2 - 22.0 * e1 - 0.5 * (gx * u[0] + gy * u[1] + gz * u[2])
    by_j = [gx - (2 / 3) * q[0], gy - (2 / 3) * q[1], gz - (2 / 3) * q[2]]
    axis, edge = -22.0 * e1 - 8.0 * e2 - by_rho, 16.0 * e1 + 2.0 * e2 - by_rho
    zero = 12.0 * e2 - 30.0 * e1 - 0.5 * by_rho
    sums = even_terms((axis, axis, axis), edge, edge, p1, q1, p2, q2, t)
    diffs = odd_terms(q, m, [-4.0 * q[a] - by_j[a] for a in range(3)], by_j)
    return turned(b, s, d, zero, sums, diffs, keep, turn)


def dot_gap(b, gap):
    parts = [b[i] * gap[i] for i in range(19)]
    while len(parts) > 1:
        parts = [a + c for a, c in zip(parts[::2], parts[1::2])] + parts[len(parts) // 2 * 2 :]
    return parts[0]


def iota(axis):
    return lax.broadcasted_iota(jnp.int32, (8, LANES), axis)


def pull(load, lane, sense, column, ring, split=False):
    z = lane & (NZ - 1)
    lower = lane < 64

    def shifted(plane, off_x, amount):
        if split:
            high, low = load(plane, 2, off_x), load(plane, 3, off_x)
            if amount == 0:
                return jnp.where(lower, high, low)
            if amount > 0:
                mixed = jnp.where(lane < 64 - amount, high, jnp.where(lane < LANES - amount, low, load(plane, 1, off_x)))
            else:
                mixed = jnp.where(lane < -amount, load(plane, 0, off_x), jnp.where(lane < 64 - amount, high, low))
            return pltpu.roll(mixed, amount % LANES, 1)
        here = load(plane, column, off_x)
        if amount == 0:
            return here
        there = load(plane, (column + (-1 if amount > 0 else 1)) % ring, off_x)
        if amount > 0:
            mixed = jnp.where(lane >= LANES - amount, there, here)
        else:
            mixed = jnp.where(lane < -amount, there, here)
        return pltpu.roll(mixed, amount % LANES, 1)

    arrived = []
    for i, (cx, cy, cz) in enumerate(VEL):
        value = shifted(i, -sense * cx, sense * (NZ * cy + cz))
        if cz != 0:
            edge = 0 if sense * cz == 1 else NZ - 1
            value = jnp.where(z == edge, shifted(OPP[i], 0, 0), value)
        arrived.append(value)
    return arrived


def counts(c):
    return (5 - c, 3 + c), (5 + c, 3 - c)


def fold_tables(low, lane):
    tables = {}
    for c in (-1, 0, 1):
        cut = jnp.where(low, NZ * (5 - c), NZ * (3 - c))
        tables[c] = cut, jnp.where(low, lane - cut, cut - 1 - lane) < 0
    return tables


def wall_layers(low):
    where = jnp.where
    return [
        (0, (where(low, 4, 5), where(low, 5, 0))), (1, (where(low, 4, 5), where(low, 6, 1))),
        (2, (where(low, 2, 3), where(low, 7, 2))), (3, (where(low, 2, 3), where(low, 5, 2))),
    ]


def first_kernel(
    snap_hbm, flag_hbm, por_hbm, adj_hbm, post_ref, adj_ref, u_ref, gap_ref, xp_ref, out_ref, in_ref, dg_ref,
    snap_ref, flag_ref, por_ref, sems,
):
    core = lax.rem(lax.axis_index("gy"), 2)
    rows = snap_ref.shape[1]
    lane, row = iota(1), iota(0)
    copies = [(flag_hbm, flag_ref), (por_hbm, por_ref)]
    copies += [(snap_hbm.at[:, 8 * g : 8 * g + 8], snap_ref.at[:, 8 * g : 8 * g + 8]) for g in range(rows // 8)]
    copies += [(adj_hbm, adj_ref)]
    copies = [pltpu.make_async_copy(src, dst, sems.at[n]) for n, (src, dst) in enumerate(copies)]
    for copy in copies:
        copy.start()
    copies[0].wait()
    copies[1].wait()
    for g in range(rows // 8):
        copies[2 + g].wait()
        at = slice(8 * g, 8 * g + 8)
        for c in range(2):
            lanes = slice(c * LANES, (c + 1) * LANES)
            kind, porous = flag_ref[at, lanes].astype(F32), por_ref[at, lanes]
            post, u, gap = collide_tile([snap_ref[i, at, lanes] for i in range(19)], coefficients(kind, porous))
            for i, value in enumerate(post + [porous, kind]):
                post_ref[i, at, lanes] = value
            for i in range(19):
                gap_ref[i, at, lanes] = gap[i]
            for a in range(3):
                u_ref[a, at, lanes] = u[a]
    copies[-1].wait()

    def plane(i, at, lanes):
        return post_ref[i, at, lanes]

    def low_spare(i, at, lanes, axis, where, unit, roll):
        value, first = plane(i, at, lanes), WALL[axis]
        extras = [(post_ref, 0, 4, 5), (post_ref, 1, 4, 6), (adj_ref, 2, 2, 7)] if i == 19 else [(adj_ref, 3, 2, 5)]
        for ref, n, layer, slot in extras:
            moved = roll(ref[first + n, at, lanes], unit * (slot - layer))
            value = jnp.where(where >= unit * slot, moved, value)
        return value

    def high_spare(i, at, lanes, axis, where, unit, roll):
        value, first = plane(i, at, lanes), WALL[axis]
        extras = [(post_ref, 2, 3, 2), (adj_ref, 1, 5, 1), (adj_ref, 0, 5, 0)] if i == 19 else [(post_ref, 3, 3, 2)]
        for ref, n, layer, slot in extras:
            moved = roll(ref[first + n, at, lanes], (unit * (slot - layer)) % (unit * 8))
            value = jnp.where(where < unit * (slot + 1), moved, value)
        return value

    def roll_rows(value, amount):
        return pltpu.roll(value, amount, 0)

    def roll_lanes(value, amount):
        return pltpu.roll(value, amount, 1)

    low_rows, high_rows = slice(0, 8), slice(rows - 8, rows)
    spare_rows, walls = [None] * 5, []
    folds = fold_tables(core == 0, lane)
    for i in range(21):
        lows, highs = [], []
        for c in range(2):
            lanes = slice(c * LANES, (c + 1) * LANES)
            if i < 19:
                (n_low, _), (_, m_high) = counts(VEL[i][0])
                low, high = plane(i, low_rows, lanes), plane(i, high_rows, lanes)
                low = jnp.where(row < n_low, low, pltpu.roll(adj_ref[i, low_rows, lanes], n_low, 0))
                high = jnp.where(row >= m_high, high, pltpu.roll(adj_ref[i, high_rows, lanes], m_high, 0))
            else:
                low = low_spare(i, low_rows, lanes, 0, row, 1, roll_rows)
                high = high_spare(i, high_rows, lanes, 0, row, 1, roll_rows)
            xp_ref[0, i, :, lanes] = low
            xp_ref[1, i, :, lanes] = high
            lows.append(low)
            highs.append(high)
        low, high = jnp.where(core == 0, *lows), jnp.where(core == 0, *highs)
        if len(dg_ref.shape) == 4:
            dg_ref[0, i], dg_ref[1, i] = low, high
        elif i >= 19:
            for n, (layer, slot) in wall_layers(core == 0):
                if (n == 3) == (i == 20):
                    kept = [pltpu.roll(t, (NZ * (slot - layer)) % LANES, 1) for t in walls[n]]
                    low, high = [jnp.where(lane // NZ == slot, k, t) for k, t in zip(kept, (low, high))]
            dg_ref[i], dg_ref[i + 2] = low, high
        else:
            if i >= WALL[1]:
                walls.append((low, high))
            cut, collided = folds[VEL[i][1]]
            own = jnp.where(row < n_low, low, high)
            other = jnp.where(row < n_low - 2, high, low)
            dg_ref[i] = jnp.where(collided, own, pltpu.roll(other, cut, 1))
            slot = 2 * (i % 4)
            moved = pltpu.roll(high, (slot - n_low + 2) % 8, 0)
            spare_rows[i // 4] = moved if slot == 0 else jnp.where(row < slot, spare_rows[i // 4], moved)
    if len(dg_ref.shape) == 3:
        for n in range(5):
            dg_ref[23 + n] = spare_rows[n]

    def pack_low(dst):
        for i in range(21):
            for g in range(rows // 8):
                at = slice(8 * g, 8 * g + 8)
                value = plane(i, at, slice(0, LANES))
                if i < 19:
                    (n, _), _ = counts(VEL[i][1])
                    value = jnp.where(lane < NZ * n, value, pltpu.roll(adj_ref[i, at, slice(0, LANES)], NZ * n, 1))
                else:
                    value = low_spare(i, at, slice(0, LANES), 1, lane, NZ, roll_lanes)
                dst[i, at, :] = value

    def pack_high(dst):
        for i in range(21):
            for g in range(rows // 8):
                at = slice(8 * g, 8 * g + 8)
                value = plane(i, at, slice(LANES, 2 * LANES))
                if i < 19:
                    _, (_, m) = counts(VEL[i][1])
                    value = jnp.where(lane >= NZ * m, value, pltpu.roll(adj_ref[i, at, slice(LANES, 2 * LANES)], NZ * m, 1))
                else:
                    value = high_spare(i, at, slice(LANES, 2 * LANES), 1, lane, NZ, roll_lanes)
                dst[i, at, :] = value

    @pl.when(core == 0)
    def _():
        pack_low(out_ref)
        pack_high(in_ref)

    @pl.when(core == 1)
    def _():
        pack_low(in_ref)
        pack_high(out_ref)


def second_kernel(
    post_in, adj_in, u0_ref, gap0_ref, xr, out_in, in_in, dg_in, xin, res_hbm, sens_hbm,
    p0, p1, p2, pe, cf, u1, u2, u3, g1, g2, g3, a4, a3, a2, a1, s1, s2, s3, res_ref, sens_ref, sems,
):
    first_core = lax.rem(lax.axis_index("gy"), 2) == 0
    rows = post_in.shape[1]
    groups = rows // 8
    lane = iota(1)
    lower = lane < 64
    roll_lanes = lambda value, amount: pltpu.roll(value, amount % LANES, 1)
    roll_rows = lambda value, amount: pltpu.roll(value, amount % 8, 0)

    def beside(i, at):
        out, inside = out_in[i, at], in_in[i, at]
        return jnp.where(first_core, inside, out), jnp.where(first_core, out, inside)

    row = iota(0)
    folds = fold_tables(jnp.logical_not(first_core), lane)
    walls = wall_layers(jnp.logical_not(first_core))

    def outer_corner(side, i):
        if len(dg_in.shape) == 4:
            return dg_in[side, i]
        if i >= 19:
            return dg_in[i + 2 * side]
        tile, n = dg_in[i], 5 - VEL[i][0]
        other = pltpu.roll(tile, LANES - folds[VEL[i][1]][0], 1)
        if side == 0:
            tile = jnp.where(row < n, tile, other)
        else:
            spare = roll_rows(dg_in[23 + i // 4], n - 2 - 2 * (i % 4))
            tile = jnp.where(row >= n, tile, jnp.where(row >= n - 2, spare, other))
        if i >= WALL[1]:
            n, (layer, slot) = walls[i - WALL[1]]
            kept = pltpu.roll(dg_in[(20 if n == 3 else 19) + 2 * side], (NZ * (layer - slot)) % LANES, 1)
            tile = jnp.where(lane // NZ == layer, kept, tile)
        return tile

    def corner(side, i):
        out, near, far = outer_corner(side, i), xin[side, i, :, 0:LANES], xin[side, i, :, LANES:]
        return jnp.where(first_core, near, out), jnp.where(first_core, out, far)

    top, bottom = slice(8 + rows, 16 + rows), slice(0, 8)
    for g in range(groups):
        at, to = slice(8 * g, 8 * g + 8), slice(8 + 8 * g, 16 + 8 * g)
        spare = {}
        for i in (19, 20) + tuple(range(19)):
            high, low = beside(i, at)
            if i >= 19:
                spare[i] = (high, low)
                pe[i - 19, to] = jnp.where(lower, high, low)
            p0[i, 0, to] = post_in[i, at, 0:LANES]
            p0[i, 1, to] = post_in[i, at, LANES:]
            n = i - WALL[1]
            p0[i, 2, to] = jnp.where(lower, high, roll_lanes(spare[19][0], -NZ * (1 + n))) if n in (0, 1) else high
            p0[i, 3, to] = jnp.where(lower, roll_lanes(spare[17 + n][1], NZ), low) if n in (2, 3) else low
            if i < 19:
                (n_low, _), (_, m_high) = counts(VEL[i][1])
                high, low = roll_lanes(high, -NZ * n_low), roll_lanes(low, -NZ * m_high)
                if n in (0, 1):
                    low = jnp.where(lane >= 96, low, roll_lanes(spare[19][1], NZ * (5 - n)))
                if n in (2, 3):
                    high = jnp.where(lane < 32, high, roll_lanes(spare[17 + n][0], -NZ * ((7, 5)[n - 2] - 2)))
                a4[i, 0, to] = adj_in[i, at, 0:LANES]
                a4[i, 1, to] = adj_in[i, at, LANES:]
                a4[i, 2, to] = jnp.where(lower, high, low)
    for side, to in ((0, top), (1, bottom)):
        for i in range(21):
            high, low = corner(side, i)
            tile = [xr[side, i, :, 0:LANES], xr[side, i, :, LANES:], high, low]
            edge = jnp.where(lower, high, low)
            for c in range(4):
                p0[i, c, to] = tile[c]
            if i >= 19:
                pe[i - 19, to] = edge
                continue
            (n_low, _), (_, m_high) = counts(VEL[i][0])
            for c, value in enumerate((tile[0], tile[1], edge)):
                a4[i, c, to] = roll_rows(value, -n_low if side == 0 else -m_high)
    moves = [(p0, 0, 19, 8 + rows + 5, 8 + rows + 4), (p0, 1, 19, 8 + rows + 6, 8 + rows + 4)]
    moves += [(a4, 2, 19, 8 + rows + 7, 8 + rows + 2), (a4, 3, 20, 8 + rows + 5, 8 + rows + 2)]
    moves += [(a4, 0, 19, 0, 5), (a4, 1, 19, 1, 5), (p0, 2, 19, 2, 3), (p0, 3, 20, 2, 3)]
    for dst, n, src, row, to in moves:
        for c in range(4):
            if dst is p0:
                dst[WALL[0] + n, c, to : to + 1] = p0[src, c, row : row + 1]
            elif c < 3:
                dst[WALL[0] + n, c, to : to + 1] = pe[src - 19, row : row + 1] if c == 2 else p0[src, c, row : row + 1]

    def fill(k, carry):
        at = pl.ds(pl.multiple_of(8 * k, 8), 8)
        for c in range(4):
            for n, value in enumerate(coefficients(p0[20, c, at], p0[19, c, at])):
                cf[n, c, at] = value
        for n in range(7):
            cf[n, 4, at] = jnp.where(lower, cf[n, 2, at], cf[n, 3, at])
        return carry

    lax.fori_loop(0, groups + 2, fill, 0, unroll=True)

    def kinds(c, cells, ring):
        column = 4 if ring == 3 and c == 2 else c
        return [cf[n, column, cells] for n in range(7)]

    def forward(src, src_base, base, n_groups, src_ring, ring, post_dst, u_dst, gap_dst):
        def body(k, carry):
            def load(i, c, off):
                return src[i, c, pl.ds(8 * k + (base - src_base + off), 8)]

            at = pl.ds(pl.multiple_of(8 * k, 8), 8)
            cells = pl.ds(8 * k + (base + 8), 8)
            sides = []
            for c in range(ring):
                f = pull(load, lane, 1, c, src_ring, src_ring != ring and c == 2)
                post, u, gap = collide_tile(f, kinds(c, cells, ring))
                if post_dst is not None:
                    for i in range(19):
                        post_dst[i, c, at] = post[i]
                if c < 2:
                    for i in range(19):
                        gap_dst[i, c, at] = gap[i]
                elif ring == 4:
                    sides.append(u)
                    if c == 2:
                        continue
                    u, c = [jnp.where(lower, a, b) for a, b in zip(*sides)], 2
                for a in range(3):
                    u_dst[a, c, at] = u[a]
            return carry

        lax.fori_loop(0, n_groups, body, 0, unroll=True)

    forward(p0, -8, -5, groups + 2, 4, 4, p1, u1, g1)
    forward(p1, -5, -4, groups + 1, 4, 3, p2, u2, g2)
    forward(p2, -4, -3, groups + 1, 3, 3, None, u3, g3)

    def backward(src, src_base, base, dst, u_src, gap_src, f_base, s_dst):
        def body(k, carry):
            def load(i, c, off):
                return src[i, c, pl.ds(8 * k + (base - src_base + off), 8)]

            at = pl.ds(pl.multiple_of(8 * k, 8), 8)
            cells = pl.ds(8 * k + (base + 8), 8)
            old = pl.ds(8 * k + (base - f_base), 8)
            for c in range(3):
                b = pull(load, lane, -1, c, 3)
                if c < 2:
                    s_dst[c, at] = dot_gap(b, [gap_src[i, c, old] for i in range(19)])
                a = adjoint_tile(b, [u_src[n, c, old] for n in range(3)], kinds(c, cells, 3))
                for i in range(19):
                    dst[i, c, at] = a[i]
            return carry

        lax.fori_loop(0, groups + 1, body, 0, unroll=True)

    backward(a4, -8, -3, a3, u3, g3, -3, s3)
    backward(a3, -3, -2, a2, u2, g2, -4, s2)
    backward(a2, -2, -1, a1, u1, g1, -5, s1)

    def results(k):
        at = pl.ds(pl.multiple_of(8 * k, 8), 8)
        return pltpu.make_async_copy(res_ref.at[:, at], res_hbm.at[:, at], sems.at[k])

    def last(k, carry):
        at = pl.ds(pl.multiple_of(8 * k, 8), 8)

        def load(i, c, off):
            return a1[i, c, pl.ds(8 * k + (1 + off), 8)]

        for c in range(2):
            lanes = slice(c * LANES, (c + 1) * LANES)
            b = pull(load, lane, -1, c, 3)
            total = dot_gap(b, [gap0_ref[i, at, lanes] for i in range(19)])
            later = s3[c, pl.ds(8 * k + 3, 8)] + s2[c, pl.ds(8 * k + 2, 8)] + s1[c, pl.ds(8 * k + 1, 8)]
            sens_ref[at, lanes] = (total + later) / (1.0 - post_in[19, at, lanes])
            a = adjoint_tile(b, [u0_ref[n, at, lanes] for n in range(3)], kinds(c, pl.ds(pl.multiple_of(8 * k + 8, 8), 8), 3))
            for i in range(19):
                res_ref[i, at, lanes] = a[i]
        results(k).start()
        return carry

    lax.fori_loop(0, groups, last, 0, unroll=True)
    sens_copy = pltpu.make_async_copy(sens_ref, sens_hbm, sems.at[groups])
    sens_copy.start()
    for k in range(groups):
        results(k).wait()
    sens_copy.wait()


VMEM = pl.BlockSpec(memory_space=pltpu.VMEM)
HBM = pl.BlockSpec(memory_space=pltpu.HBM)


def exchange(xp, out, inside, dg):
    nx, ny = lax.axis_size("gx"), lax.axis_size("gy")
    same = [(i, i ^ 1) for i in range(ny)]
    other = [(i, (i + 1) % ny if i % 2 else (i - 1) % ny) for i in range(ny)]

    def along(value, axes, pairs_of):
        if nx == 2:
            return lax.ppermute(value, axes, pairs_of(1))
        return jnp.stack([lax.ppermute(value[0], axes, pairs_of(-1)), lax.ppermute(value[1], axes, pairs_of(1))])

    xr = along(xp, "gx", lambda step: [(i, (i + step) % nx) for i in range(nx)])
    out_r = lax.ppermute(out, "gy", other)
    dg_r = along(
        dg, ("gx", "gy"), lambda step: [(i * ny + j, ((i + step) % nx) * ny + k) for i in range(nx) for j, k in other]
    )
    in_r = lax.ppermute(inside, "gy", same)
    xr, out_r, dg_r, in_r = lax.optimization_barrier((xr, out_r, dg_r, in_r))
    xin = lax.ppermute(xr, "gy", same)
    return xr, out_r, in_r, dg_r, xin


def per_device(snapshot, flags, porosity, adjoint_end):
    _, rows, lanes = snapshot.shape
    assert lanes == 2 * LANES and rows % 8 == 0

    def array(*shape):
        return jax.ShapeDtypeStruct(shape, F32)

    def scratch(*shape):
        return pltpu.VMEM(shape, F32)

    groups = rows // 8
    post, adj, u0, gap0, xp, out, inside, dg = pl.pallas_call(
        first_kernel,
        out_shape=(
            array(21, rows, lanes), array(19, rows, lanes), array(3, rows, lanes), array(19, rows, lanes),
            array(2, 21, 8, lanes), array(21, rows, LANES), array(21, rows, LANES),
            array(*((28,) if lax.axis_size("gx") == 2 else (2, 21)), 8, LANES),
        ),
        in_specs=[HBM] * 4,
        out_specs=(VMEM,) * 8,
        scratch_shapes=[
            scratch(19, rows, lanes), pltpu.VMEM((rows, lanes), jnp.int32), scratch(rows, lanes),
            pltpu.SemaphoreType.DMA((groups + 3,)),
        ],
        compiler_params=pltpu.CompilerParams(vmem_limit_bytes=12 << 20),
        name="collide_and_pack",
    )(*[pltpu.with_memory_space_constraint(v, pltpu.HBM) for v in (snapshot, flags, porosity, adjoint_end)])
    received = exchange(xp, out, inside, dg)
    tall, mid = rows + 24, rows + 16
    return pl.pallas_call(
        second_kernel,
        out_shape=(array(19, rows, lanes), array(rows, lanes)),
        in_specs=[VMEM] * 9,
        out_specs=(HBM, HBM),
        scratch_shapes=[
            scratch(21, 4, tall, LANES), scratch(19, 4, tall, LANES), scratch(19, 3, tall, LANES), scratch(2, tall, LANES),
            scratch(7, 5, tall, LANES),
            scratch(3, 3, mid, LANES), scratch(3, 3, mid, LANES), scratch(3, 3, mid, LANES),
            scratch(19, 2, mid, LANES), scratch(19, 2, mid, LANES), scratch(19, 2, mid, LANES),
            scratch(19, 3, mid, LANES), scratch(19, 3, mid, LANES), scratch(19, 3, mid, LANES), scratch(19, 3, mid, LANES),
            scratch(2, mid, LANES), scratch(2, mid, LANES), scratch(2, mid, LANES),
            scratch(19, rows, lanes), scratch(rows, lanes), pltpu.SemaphoreType.DMA((groups + 1,)),
        ],
        compiler_params=pltpu.CompilerParams(vmem_limit_bytes=28 << 20),
        name="window",
    )(post, adj, u0, gap0, *received)


def solution(mesh):
    placed = (P(None, "gx", "gy"), P("gx", "gy"), P("gx", "gy"), P(None, "gx", "gy"))
    return jax.shard_map(
        per_device,
        mesh=mesh,
        in_specs=placed,
        out_specs=(P(None, "gx", "gy"), P("gx", "gy")),
        check_vma=False,
    )
```

```python
import jax
import jax.numpy as jnp
from jax import lax
from jax.experimental import pallas as pl
from jax.experimental.pallas import tpu as pltpu
from jax.sharding import PartitionSpec as P

NZ = 16
LANES = 128
F32 = jnp.float32


def velocity_list():
    found = [(0, 0, 0)]
    for axis in range(3):
        for sense in (1, -1):
            vector = [0, 0, 0]
            vector[axis] = sense
            found.append(tuple(vector))
    for a, b in ((0, 1), (0, 2), (1, 2)):
        for sense_a in (1, -1):
            for sense_b in (1, -1):
                vector = [0, 0, 0]
                vector[a], vector[b] = sense_a, sense_b
                found.append(tuple(vector))
    return found


VEL = velocity_list()
OPP = [VEL.index(tuple(-v for v in c)) for c in VEL]
PAIRS = [(1, 2), (3, 4), (5, 6), (7, 10), (8, 9), (11, 14), (12, 13), (15, 18), (16, 17)]
R_E, R_EPS, R_Q, R_NU, R_PI, R_M = 1.19, 1.4, 1.2, 1.0 / 0.6, 1.4, 1.98
WALL = (11, 15)
IN_CX, IN_NO = 1 + 0.01125 - 0.00375, 1 - 0.00375


def coefficients(kind, porous):
    half = 0.5 * (1.0 - porous)
    fluid, outlet, inlet, wall = kind == 0.0, kind == 3.0, kind == 2.0, kind == 1.0
    none = jnp.zeros_like(half)

    def rate(value, scale):
        return half * jnp.where(fluid, value * scale, jnp.where(outlet, scale, 0.0)).astype(F32)

    return [
        rate(R_E, 1 / 126), rate(R_EPS, 1 / 252), rate(R_NU, 1 / 18), rate(R_Q, 1 / 12), rate(R_M, 1 / 4),
        0.5 - jnp.where(inlet, half, none),
        jnp.where(wall, none, jnp.where(inlet, half, half + half)) - 0.5,
    ]


def moments(f):
    s = [f[a] + f[b] for a, b in PAIRS]
    d = [f[a] - f[b] for a, b in PAIRS]
    big_s = [s[3] + s[4], s[5] + s[6], s[7] + s[8]]
    off = [s[3] - s[4], s[5] - s[6], s[7] - s[8]]
    ex, gy = d[3] + d[4], d[3] - d[4]
    gx, ez = d[5] + d[6], d[5] - d[6]
    ey, gz = d[7] + d[8], d[7] - d[8]
    return s, d, big_s, off, (ex, ey, ez), (gx, gy, gz)


def even_terms(axis, edge, edge_yz, p1, q1, p2, q2, t):
    a1, b1, a2, b2 = p1 - 2.0 * q1, p1 + q1, p2 - 2.0 * q2, p2 + q2
    xy, xz, yz = edge + b1 + b2, edge + b1 - b2, edge_yz - 2.0 * b1
    return [
        axis[0] + 2.0 * a1, axis[1] - a1 + a2, axis[2] - a1 - a2,
        xy + t[0], xy - t[0], xz + t[1], xz - t[1], yz + t[2], yz - t[2],
    ]


def odd_terms(q, m, along, less):
    base = [q[a] if less[a] is None else q[a] - less[a] for a in range(3)]
    pos, neg = [base[a] + m[a] for a in range(3)], [base[a] - m[a] for a in range(3)]
    return along + [
        pos[0] + neg[1], pos[0] - neg[1], neg[0] + pos[2], neg[0] - pos[2], pos[1] + neg[2], pos[1] - neg[2],
    ]


def turned(f, s, d, zero, sums, diffs, keep, turn):
    out = [None] * 19
    out[0] = 2.0 * (keep * f[0] - zero)
    for n, (a, b) in enumerate(PAIRS):
        even, odd = keep * s[n] - sums[n], turn * d[n] - diffs[n]
        out[a], out[b] = even + odd, even - odd
    return out


def collide_tile(f, coefs):
    c_e, c_eps, c_nu, c_q, c_m, keep, turn = coefs
    s, d, big, off, e, g = moments(f)
    axis_sum = s[0] + s[1] + s[2]
    edge_sum = big[0] + big[1] + big[2]
    rho = f[0] + axis_sum + edge_sum
    eg = [e[a] + g[a] for a in range(3)]
    j = [d[a] + eg[a] for a in range(3)]
    inv = 1.0 / rho
    u = [j[a] * inv for a in range(3)]
    xx, yy, zz = j[0] * u[0], j[1] * u[1], j[2] * u[2]
    energy = xx + yy + zz
    e1 = c_e * (edge_sum - f[0] - energy)
    e2 = c_eps * (9.0 * f[0] - 7.0 * axis_sum - 2.0 * edge_sum + 5.5 * energy)
    yz_a, yz_e, yz_u = s[1] - s[2], big[0] - big[1], yy - zz
    x_a = 2.0 * s[0] - (s[1] + s[2])
    x_e = big[0] + big[1] - 2.0 * big[2]
    x_u = 2.0 * xx - (yy + zz)
    p1 = c_nu * (x_a + x_e - x_u)
    q1 = (7.0 * c_eps) * (x_e - 2.0 * x_a + 0.5 * x_u)
    p2 = (3.0 * c_nu) * (yz_a + yz_e - yz_u)
    q2 = (21.0 * c_eps) * (yz_e - 2.0 * yz_a + 0.5 * yz_u)
    c_off = 9.0 * c_nu
    t = [c_off * (off[0] - j[0] * u[1]), c_off * (off[1] - j[0] * u[2]), c_off * (off[2] - j[1] * u[2])]
    q = [c_q * (eg[a] - 2.0 * d[a]) for a in range(3)]
    m = [c_m * (e[a] - g[a]) for a in range(3)]
    inlet = 0.5 - keep
    axis, edge = -22.0 * e1 - 8.0 * e2, 16.0 * e1 + 2.0 * e2
    zero = 12.0 * e2 - 30.0 * e1 - inlet * (IN_NO / 3)
    axis_yz = axis - inlet * (IN_NO / 9)
    sums = even_terms(
        (axis - inlet * (IN_CX / 9), axis_yz, axis_yz), edge - inlet * (IN_CX / 18), edge - inlet * (IN_NO / 18), p1, q1, p2, q2, t
    )
    along = [-4.0 * q[0] - inlet * (0.15 / 9), -4.0 * q[1], -4.0 * q[2]]
    diffs = odd_terms(q, m, along, (inlet * (0.15 / 18), None, None))
    post = turned(f, s, d, zero, sums, diffs, keep, turn)
    return post, u, [f[OPP[i]] - post[i] for i in range(19)]


def adjoint_tile(b, u, coefs):
    c_e, c_eps, c_nu, c_q, c_m, keep, turn = coefs
    s, d, big, off, e, g = moments(b)
    axis_sum = s[0] + s[1] + s[2]
    edge_sum = big[0] + big[1] + big[2]
    eg = [e[a] + g[a] for a in range(3)]
    e1 = c_e * ((8 / 19) * edge_sum - (11 / 19) * axis_sum - (30 / 19) * b[0])
    e2 = c_eps * (12.0 * b[0] - 4.0 * axis_sum + edge_sum)
    yz_a, yz_e = s[1] - s[2], big[0] - big[1]
    x_a = 2.0 * s[0] - (s[1] + s[2])
    x_e = big[0] + big[1] - 2.0 * big[2]
    p1 = c_nu * (x_a + x_e)
    q1 = (7.0 * c_eps) * (x_e - 2.0 * x_a)
    p2 = (3.0 * c_nu) * (yz_a + yz_e)
    q2 = (21.0 * c_eps) * (yz_e - 2.0 * yz_a)
    c_off = 9.0 * c_nu
    t = [c_off * off[n] for n in range(3)]
    q = [c_q * (0.6 * eg[a] - 2.4 * d[a]) for a in range(3)]
    m = [c_m * (e[a] - g[a]) for a in range(3)]
    common = 76.0 * e1 - 22.0 * e2
    v, w = 2.0 * p1 - q1, 2.0 * p2 - q2
    less_v = common - v
    k = [common + 2.0 * v, less_v + w, less_v - w]
    gx = k[0] * u[0] + t[0] * u[1] + t[1] * u[2]
    gy = k[1] * u[1] + t[0] * u[0] + t[2] * u[2]
    gz = k[2] * u[2] + t[1] * u[0] + t[2] * u[1]
    by_rho = 6.0 * e2 - 22.0 * e1 - 0.5 * (gx * u[0] + gy * u[1] + gz * u[2])
    by_j = [gx - (2 / 3) * q[0], gy - (2 / 3) * q[1], gz - (2 / 3) * q[2]]
    axis, edge = -22.0 * e1 - 8.0 * e2 - by_rho, 16.0 * e1 + 2.0 * e2 - by_rho
    zero = 12.0 * e2 - 30.0 * e1 - 0.5 * by_rho
    sums = even_terms((axis, axis, axis), edge, edge, p1, q1, p2, q2, t)
    diffs = odd_terms(q, m, [-4.0 * q[a] - by_j[a] for a in range(3)], by_j)
    return turned(b, s, d, zero, sums, diffs, keep, turn)


def dot_gap(b, gap):
    parts = [b[i] * gap[i] for i in range(19)]
    while len(parts) > 1:
        parts = [a + c for a, c in zip(parts[::2], parts[1::2])] + parts[len(parts) // 2 * 2 :]
    return parts[0]


def iota(axis):
    return lax.broadcasted_iota(jnp.int32, (8, LANES), axis)


def pull(load, lane, sense, column, ring, split=False):
    z = lane & (NZ - 1)
    lower = lane < 64

    def shifted(plane, off_x, along_y, amount):
        if split:
            high, low = load(plane, 2, off_x), load(plane, 3, off_x)
            if along_y == 0:
                mixed = jnp.where(lower, high, low)
            elif along_y > 0:
                mixed = jnp.where(lane < 64 - NZ, high, jnp.where(lane < LANES - NZ, low, load(plane, 1, off_x)))
            else:
                mixed = jnp.where(lane < NZ, load(plane, 0, off_x), jnp.where(lane < 64 + NZ, high, low))
        else:
            mixed = load(plane, column, off_x)
            if along_y != 0:
                there = load(plane, (column - along_y) % ring, off_x)
                mixed = jnp.where(lane >= LANES - NZ if along_y > 0 else lane < NZ, there, mixed)
        return pltpu.roll(mixed, amount % LANES, 1) if amount != 0 else mixed

    arrived = []
    for i, (cx, cy, cz) in enumerate(VEL):
        value = shifted(i, -sense * cx, sense * cy, sense * (NZ * cy + cz))
        if cz != 0:
            edge = 0 if sense * cz == 1 else NZ - 1
            value = jnp.where(z == edge, shifted(OPP[i], 0, 0, 0), value)
        arrived.append(value)
    return arrived


def counts(c):
    return (5 - c, 3 + c), (5 + c, 3 - c)


def fold_tables(low, lane):
    tables = {}
    for c in (-1, 0, 1):
        cut = jnp.where(low, NZ * (5 - c), NZ * (3 - c))
        tables[c] = cut, jnp.where(low, lane - cut, cut - 1 - lane) < 0
    return tables


def wall_layers(low):
    where = jnp.where
    return [
        (0, (where(low, 4, 5), where(low, 5, 0))), (1, (where(low, 4, 5), where(low, 6, 1))),
        (2, (where(low, 2, 3), where(low, 7, 2))), (3, (where(low, 2, 3), where(low, 5, 2))),
    ]


def first_kernel(
    snap_hbm, flag_hbm, por_hbm, adj_hbm, post_ref, adj_ref, u_ref, gap_ref, xp_ref, out_ref, in_ref, dg_ref,
    snap_ref, flag_ref, por_ref, sems,
):
    core = lax.rem(lax.axis_index("gy"), 2)
    rows = snap_ref.shape[1]
    lane, row = iota(1), iota(0)
    groups = rows // 8
    order = [0, groups - 1] + list(range(1, groups - 1))
    copies = [(flag_hbm, flag_ref), (por_hbm, por_ref), (adj_hbm, adj_ref)]
    copies += [(snap_hbm.at[:, 8 * g : 8 * g + 8], snap_ref.at[:, 8 * g : 8 * g + 8]) for g in order]
    copies = [pltpu.make_async_copy(src, dst, sems.at[n]) for n, (src, dst) in enumerate(copies)]
    for copy in copies:
        copy.start()
    for copy in copies[:3]:
        copy.wait()

    def collide_rows(g):
        copies[3 + order.index(g)].wait()
        at = slice(8 * g, 8 * g + 8)
        for c in range(2):
            lanes = slice(c * LANES, (c + 1) * LANES)
            kind, porous = flag_ref[at, lanes].astype(F32), por_ref[at, lanes]
            post, u, gap = collide_tile([snap_ref[i, at, lanes] for i in range(19)], coefficients(kind, porous))
            for i, value in enumerate(post + [porous, kind]):
                post_ref[i, at, lanes] = value
            for i in range(19):
                gap_ref[i, at, lanes] = gap[i]
            for a in range(3):
                u_ref[a, at, lanes] = u[a]

    def plane(i, at, lanes):
        return post_ref[i, at, lanes]

    def low_spare(i, at, lanes, axis, where, unit, roll):
        value, first = plane(i, at, lanes), WALL[axis]
        extras = [(post_ref, 0, 4, 5), (post_ref, 1, 4, 6), (adj_ref, 2, 2, 7)] if i == 19 else [(adj_ref, 3, 2, 5)]
        for ref, n, layer, slot in extras:
            moved = roll(ref[first + n, at, lanes], unit * (slot - layer))
            value = jnp.where(where >= unit * slot, moved, value)
        return value

    def high_spare(i, at, lanes, axis, where, unit, roll):
        value, first = plane(i, at, lanes), WALL[axis]
        extras = [(post_ref, 2, 3, 2), (adj_ref, 1, 5, 1), (adj_ref, 0, 5, 0)] if i == 19 else [(post_ref, 3, 3, 2)]
        for ref, n, layer, slot in extras:
            moved = roll(ref[first + n, at, lanes], (unit * (slot - layer)) % (unit * 8))
            value = jnp.where(where < unit * (slot + 1), moved, value)
        return value

    def roll_rows(value, amount):
        return pltpu.roll(value, amount, 0)

    def roll_lanes(value, amount):
        return pltpu.roll(value, amount, 1)

    first_core = core == 0

    def pack_rows(g):
        at = slice(8 * g, 8 * g + 8)
        left, right = slice(0, LANES), slice(LANES, 2 * LANES)
        for i in range(21):
            if i < 19:
                (n, _), (_, m) = counts(VEL[i][1])
                low = jnp.where(lane < NZ * n, plane(i, at, left), pltpu.roll(adj_ref[i, at, left], NZ * n, 1))
                high = jnp.where(lane >= NZ * m, plane(i, at, right), pltpu.roll(adj_ref[i, at, right], NZ * m, 1))
            else:
                low = low_spare(i, at, left, 1, lane, NZ, roll_lanes)
                high = high_spare(i, at, right, 1, lane, NZ, roll_lanes)
            out_ref[i, at, :] = jnp.where(first_core, low, high)
            in_ref[i, at, :] = jnp.where(first_core, high, low)

    for g in order[:2]:
        collide_rows(g)
        pack_rows(g)
    low_rows, high_rows = slice(0, 8), slice(rows - 8, rows)
    spare_rows, walls = [None] * 5, []
    folds = fold_tables(core == 0, lane)
    for i in range(21):
        lows, highs = [], []
        for c in range(2):
            lanes = slice(c * LANES, (c + 1) * LANES)
            if i < 19:
                (n_low, _), (_, m_high) = counts(VEL[i][0])
                low, high = plane(i, low_rows, lanes), plane(i, high_rows, lanes)
                low = jnp.where(row < n_low, low, pltpu.roll(adj_ref[i, low_rows, lanes], n_low, 0))
                high = jnp.where(row >= m_high, high, pltpu.roll(adj_ref[i, high_rows, lanes], m_high, 0))
            else:
                low = low_spare(i, low_rows, lanes, 0, row, 1, roll_rows)
                high = high_spare(i, high_rows, lanes, 0, row, 1, roll_rows)
            xp_ref[0, i, :, lanes] = low
            xp_ref[1, i, :, lanes] = high
            lows.append(low)
            highs.append(high)
        low, high = jnp.where(core == 0, *lows), jnp.where(core == 0, *highs)
        if len(dg_ref.shape) == 4:
            dg_ref[0, i], dg_ref[1, i] = low, high
        elif i >= 19:
            for n, (layer, slot) in wall_layers(core == 0):
                if (n == 3) == (i == 20):
                    kept = [pltpu.roll(t, (NZ * (slot - layer)) % LANES, 1) for t in walls[n]]
                    low, high = [jnp.where(lane // NZ == slot, k, t) for k, t in zip(kept, (low, high))]
            dg_ref[i], dg_ref[i + 2] = low, high
        else:
            if i >= WALL[1]:
                walls.append((low, high))
            cut, collided = folds[VEL[i][1]]
            own = jnp.where(row < n_low, low, high)
            other = jnp.where(row < n_low - 2, high, low)
            dg_ref[i] = jnp.where(collided, own, pltpu.roll(other, cut, 1))
            slot = 2 * (i % 4)
            moved = pltpu.roll(high, (slot - n_low + 2) % 8, 0)
            spare_rows[i // 4] = moved if slot == 0 else jnp.where(row < slot, spare_rows[i // 4], moved)
    if len(dg_ref.shape) == 3:
        for n in range(5):
            dg_ref[23 + n] = spare_rows[n]
    for g in order[2:]:
        collide_rows(g)
        pack_rows(g)


def second_kernel(
    post_in, adj_in, u0_ref, gap0_ref, xr, out_in, in_in, dg_in, xin, res_hbm, sens_hbm,
    p0, p1, p2, pe, cf, u1, u2, u3, g1, g2, g3, a4, a3, a2, a1, s1, s2, s3, res_ref, sens_ref, sems,
):
    first_core = lax.rem(lax.axis_index("gy"), 2) == 0
    rows = post_in.shape[1]
    groups = rows // 8
    lane = iota(1)
    lower = lane < 64
    roll_lanes = lambda value, amount: pltpu.roll(value, amount % LANES, 1)
    roll_rows = lambda value, amount: pltpu.roll(value, amount % 8, 0)

    def beside(i, at):
        out, inside = out_in[i, at], in_in[i, at]
        return jnp.where(first_core, inside, out), jnp.where(first_core, out, inside)

    row = iota(0)
    folds = fold_tables(jnp.logical_not(first_core), lane)
    walls = wall_layers(jnp.logical_not(first_core))

    def outer_corner(side, i):
        if len(dg_in.shape) == 4:
            return dg_in[side, i]
        if i >= 19:
            return dg_in[i + 2 * side]
        tile, n = dg_in[i], 5 - VEL[i][0]
        other = pltpu.roll(tile, LANES - folds[VEL[i][1]][0], 1)
        if side == 0:
            tile = jnp.where(row < n, tile, other)
        else:
            spare = roll_rows(dg_in[23 + i // 4], n - 2 - 2 * (i % 4))
            tile = jnp.where(row >= n, tile, jnp.where(row >= n - 2, spare, other))
        if i >= WALL[1]:
            n, (layer, slot) = walls[i - WALL[1]]
            kept = pltpu.roll(dg_in[(20 if n == 3 else 19) + 2 * side], (NZ * (layer - slot)) % LANES, 1)
            tile = jnp.where(lane // NZ == layer, kept, tile)
        return tile

    def corner(side, i):
        out, near, far = outer_corner(side, i), xin[side, i, :, 0:LANES], xin[side, i, :, LANES:]
        return jnp.where(first_core, near, out), jnp.where(first_core, out, far)

    top, bottom = slice(8 + rows, 16 + rows), slice(0, 8)
    for g in range(groups):
        at, to = slice(8 * g, 8 * g + 8), slice(8 + 8 * g, 16 + 8 * g)
        spare = {}
        for i in (19, 20) + tuple(range(19)):
            high, low = beside(i, at)
            if i >= 19:
                spare[i] = (high, low)
                pe[i - 19, to] = jnp.where(lower, high, low)
            p0[i, 0, to] = post_in[i, at, 0:LANES]
            p0[i, 1, to] = post_in[i, at, LANES:]
            n = i - WALL[1]
            p0[i, 2, to] = jnp.where(lower, high, roll_lanes(spare[19][0], -NZ * (1 + n))) if n in (0, 1) else high
            p0[i, 3, to] = jnp.where(lower, roll_lanes(spare[17 + n][1], NZ), low) if n in (2, 3) else low
            if i < 19:
                (n_low, _), (_, m_high) = counts(VEL[i][1])
                high, low = roll_lanes(high, -NZ * n_low), roll_lanes(low, -NZ * m_high)
                if n in (0, 1):
                    low = jnp.where(lane >= 96, low, roll_lanes(spare[19][1], NZ * (5 - n)))
                if n in (2, 3):
                    high = jnp.where(lane < 32, high, roll_lanes(spare[17 + n][0], -NZ * ((7, 5)[n - 2] - 2)))
                a4[i, 0, to] = adj_in[i, at, 0:LANES]
                a4[i, 1, to] = adj_in[i, at, LANES:]
                a4[i, 2, to] = jnp.where(lower, high, low)
    for side, to in ((0, top), (1, bottom)):
        for i in range(21):
            high, low = corner(side, i)
            tile = [xr[side, i, :, 0:LANES], xr[side, i, :, LANES:], high, low]
            edge = jnp.where(lower, high, low)
            for c in range(4):
                p0[i, c, to] = tile[c]
            if i >= 19:
                pe[i - 19, to] = edge
                continue
            (n_low, _), (_, m_high) = counts(VEL[i][0])
            for c, value in enumerate((tile[0], tile[1], edge)):
                a4[i, c, to] = roll_rows(value, -n_low if side == 0 else -m_high)
    moves = [(p0, 0, 19, 8 + rows + 5, 8 + rows + 4), (p0, 1, 19, 8 + rows + 6, 8 + rows + 4)]
    moves += [(a4, 2, 19, 8 + rows + 7, 8 + rows + 2), (a4, 3, 20, 8 + rows + 5, 8 + rows + 2)]
    moves += [(a4, 0, 19, 0, 5), (a4, 1, 19, 1, 5), (p0, 2, 19, 2, 3), (p0, 3, 20, 2, 3)]
    for dst, n, src, row, to in moves:
        for c in range(4):
            if dst is p0:
                dst[WALL[0] + n, c, to : to + 1] = p0[src, c, row : row + 1]
            elif c < 3:
                dst[WALL[0] + n, c, to : to + 1] = pe[src - 19, row : row + 1] if c == 2 else p0[src, c, row : row + 1]

    def fill(k, carry):
        at = pl.ds(pl.multiple_of(8 * k, 8), 8)
        for c in range(4):
            for n, value in enumerate(coefficients(p0[20, c, at], p0[19, c, at])):
                cf[n, c, at] = value
        for n in range(7):
            cf[n, 4, at] = jnp.where(lower, cf[n, 2, at], cf[n, 3, at])
        return carry

    lax.fori_loop(0, groups + 2, fill, 0, unroll=True)

    def kinds(c, cells, ring):
        column = 4 if ring == 3 and c == 2 else c
        return [cf[n, column, cells] for n in range(7)]

    def forward(src, src_base, base, n_groups, src_ring, ring, post_dst, u_dst, gap_dst):
        def body(k, carry):
            def load(i, c, off):
                return src[i, c, pl.ds(8 * k + (base - src_base + off), 8)]

            at = pl.ds(pl.multiple_of(8 * k, 8), 8)
            cells = pl.ds(8 * k + (base + 8), 8)
            sides = []
            for c in range(ring):
                f = pull(load, lane, 1, c, src_ring, src_ring != ring and c == 2)
                post, u, gap = collide_tile(f, kinds(c, cells, ring))
                if post_dst is not None:
                    for i in range(19):
                        post_dst[i, c, at] = post[i]
                if c < 2:
                    for i in range(19):
                        gap_dst[i, c, at] = gap[i]
                elif ring == 4:
                    sides.append(u)
                    if c == 2:
                        continue
                    u, c = [jnp.where(lower, a, b) for a, b in zip(*sides)], 2
                for a in range(3):
                    u_dst[a, c, at] = u[a]
            return carry

        lax.fori_loop(0, n_groups, body, 0, unroll=True)

    forward(p0, -8, -5, groups + 2, 4, 4, p1, u1, g1)
    forward(p1, -5, -4, groups + 1, 4, 3, p2, u2, g2)
    forward(p2, -4, -3, groups + 1, 3, 3, None, u3, g3)

    def backward(src, src_base, base, dst, u_src, gap_src, f_base, s_dst):
        def body(k, carry):
            def load(i, c, off):
                return src[i, c, pl.ds(8 * k + (base - src_base + off), 8)]

            at = pl.ds(pl.multiple_of(8 * k, 8), 8)
            cells = pl.ds(8 * k + (base + 8), 8)
            old = pl.ds(8 * k + (base - f_base), 8)
            for c in range(3):
                b = pull(load, lane, -1, c, 3)
                if c < 2:
                    s_dst[c, at] = dot_gap(b, [gap_src[i, c, old] for i in range(19)])
                a = adjoint_tile(b, [u_src[n, c, old] for n in range(3)], kinds(c, cells, 3))
                for i in range(19):
                    dst[i, c, at] = a[i]
            return carry

        lax.fori_loop(0, groups + 1, body, 0, unroll=True)

    backward(a4, -8, -3, a3, u3, g3, -3, s3)
    backward(a3, -3, -2, a2, u2, g2, -4, s2)
    backward(a2, -2, -1, a1, u1, g1, -5, s1)

    def results(k):
        at = pl.ds(pl.multiple_of(8 * k, 8), 8)
        return pltpu.make_async_copy(res_ref.at[:, at], res_hbm.at[:, at], sems.at[k])

    def last(k, carry):
        at = pl.ds(pl.multiple_of(8 * k, 8), 8)

        def load(i, c, off):
            return a1[i, c, pl.ds(8 * k + (1 + off), 8)]

        for c in range(2):
            lanes = slice(c * LANES, (c + 1) * LANES)
            b = pull(load, lane, -1, c, 3)
            total = dot_gap(b, [gap0_ref[i, at, lanes] for i in range(19)])
            later = s3[c, pl.ds(8 * k + 3, 8)] + s2[c, pl.ds(8 * k + 2, 8)] + s1[c, pl.ds(8 * k + 1, 8)]
            sens_ref[at, lanes] = (total + later) / (1.0 - post_in[19, at, lanes])
            a = adjoint_tile(b, [u0_ref[n, at, lanes] for n in range(3)], kinds(c, pl.ds(pl.multiple_of(8 * k + 8, 8), 8), 3))
            for i in range(19):
                res_ref[i, at, lanes] = a[i]
        results(k).start()
        return carry

    lax.fori_loop(0, groups, last, 0, unroll=True)
    sens_copy = pltpu.make_async_copy(sens_ref, sens_hbm, sems.at[groups])
    sens_copy.start()
    for k in range(groups):
        results(k).wait()
    sens_copy.wait()


VMEM = pl.BlockSpec(memory_space=pltpu.VMEM)
HBM = pl.BlockSpec(memory_space=pltpu.HBM)


def exchange(xp, out, inside, dg):
    nx, ny = lax.axis_size("gx"), lax.axis_size("gy")
    same = [(i, i ^ 1) for i in range(ny)]
    other = [(i, (i + 1) % ny if i % 2 else (i - 1) % ny) for i in range(ny)]

    def along(value, axes, pairs_of):
        if nx == 2:
            return lax.ppermute(value, axes, pairs_of(1))
        return jnp.stack([lax.ppermute(value[0], axes, pairs_of(-1)), lax.ppermute(value[1], axes, pairs_of(1))])

    xr = along(xp, "gx", lambda step: [(i, (i + step) % nx) for i in range(nx)])
    out_r = lax.ppermute(out, "gy", other)
    dg_r = along(
        dg, ("gx", "gy"), lambda step: [(i * ny + j, ((i + step) % nx) * ny + k) for i in range(nx) for j, k in other]
    )
    in_r = lax.ppermute(inside, "gy", same)
    xr, out_r, dg_r, in_r = lax.optimization_barrier((xr, out_r, dg_r, in_r))
    xin = lax.ppermute(xr, "gy", same)
    return xr, out_r, in_r, dg_r, xin


def per_device(snapshot, flags, porosity, adjoint_end):
    _, rows, lanes = snapshot.shape
    assert lanes == 2 * LANES and rows % 8 == 0

    def array(*shape):
        return jax.ShapeDtypeStruct(shape, F32)

    def scratch(*shape):
        return pltpu.VMEM(shape, F32)

    groups = rows // 8
    post, adj, u0, gap0, xp, out, inside, dg = pl.pallas_call(
        first_kernel,
        out_shape=(
            array(21, rows, lanes), array(19, rows, lanes), array(3, rows, lanes), array(19, rows, lanes),
            array(2, 21, 8, lanes), array(21, rows, LANES), array(21, rows, LANES),
            array(*((28,) if lax.axis_size("gx") == 2 else (2, 21)), 8, LANES),
        ),
        in_specs=[HBM] * 4,
        out_specs=(VMEM,) * 8,
        scratch_shapes=[
            scratch(19, rows, lanes), pltpu.VMEM((rows, lanes), jnp.int32), scratch(rows, lanes),
            pltpu.SemaphoreType.DMA((groups + 3,)),
        ],
        compiler_params=pltpu.CompilerParams(vmem_limit_bytes=12 << 20),
        name="collide_and_pack",
    )(*[pltpu.with_memory_space_constraint(v, pltpu.HBM) for v in (snapshot, flags, porosity, adjoint_end)])
    received = exchange(xp, out, inside, dg)
    tall, mid = rows + 24, rows + 16
    return pl.pallas_call(
        second_kernel,
        out_shape=(array(19, rows, lanes), array(rows, lanes)),
        in_specs=[VMEM] * 9,
        out_specs=(HBM, HBM),
        scratch_shapes=[
            scratch(21, 4, tall, LANES), scratch(19, 4, tall, LANES), scratch(19, 3, tall, LANES), scratch(2, tall, LANES),
            scratch(7, 5, tall, LANES),
            scratch(3, 3, mid, LANES), scratch(3, 3, mid, LANES), scratch(3, 3, mid, LANES),
            scratch(19, 2, mid, LANES), scratch(19, 2, mid, LANES), scratch(19, 2, mid, LANES),
            scratch(19, 3, mid, LANES), scratch(19, 3, mid, LANES), scratch(19, 3, mid, LANES), scratch(19, 3, mid, LANES),
            scratch(2, mid, LANES), scratch(2, mid, LANES), scratch(2, mid, LANES),
            scratch(19, rows, lanes), scratch(rows, lanes), pltpu.SemaphoreType.DMA((groups + 1,)),
        ],
        compiler_params=pltpu.CompilerParams(vmem_limit_bytes=28 << 20),
        name="window",
    )(post, adj, u0, gap0, *received)


def solution(mesh):
    placed = (P(None, "gx", "gy"), P("gx", "gy"), P("gx", "gy"), P(None, "gx", "gy"))
    return jax.shard_map(
        per_device,
        mesh=mesh,
        in_specs=placed,
        out_specs=(P(None, "gx", "gy"), P("gx", "gy")),
        check_vma=False,
    )
```

```python
import jax
import jax.numpy as jnp
from jax import lax
from jax.experimental import pallas as pl
from jax.experimental.pallas import tpu as pltpu
from jax.sharding import PartitionSpec as P

NZ = 16
LANES = 128
F32 = jnp.float32


def velocity_list():
    found = [(0, 0, 0)]
    for axis in range(3):
        for sense in (1, -1):
            vector = [0, 0, 0]
            vector[axis] = sense
            found.append(tuple(vector))
    for a, b in ((0, 1), (0, 2), (1, 2)):
        for sense_a in (1, -1):
            for sense_b in (1, -1):
                vector = [0, 0, 0]
                vector[a], vector[b] = sense_a, sense_b
                found.append(tuple(vector))
    return found


VEL = velocity_list()
OPP = [VEL.index(tuple(-v for v in c)) for c in VEL]
PAIRS = [(1, 2), (3, 4), (5, 6), (7, 10), (8, 9), (11, 14), (12, 13), (15, 18), (16, 17)]
R_E, R_EPS, R_Q, R_NU, R_PI, R_M = 1.19, 1.4, 1.2, 1.0 / 0.6, 1.4, 1.98
WALL = (11, 15)
IN_CX, IN_NO = 1 + 0.01125 - 0.00375, 1 - 0.00375


def coefficients(kind, porous):
    half = 0.5 * (1.0 - porous)
    fluid, outlet, inlet, wall = kind == 0.0, kind == 3.0, kind == 2.0, kind == 1.0
    none = jnp.zeros_like(half)

    def rate(value, scale):
        return half * jnp.where(fluid, value * scale, jnp.where(outlet, scale, 0.0)).astype(F32)

    return [
        rate(R_E, 1 / 126), rate(R_EPS, 1 / 252), rate(R_NU, 1 / 18), rate(R_Q, 1 / 12), rate(R_M, 1 / 4),
        0.5 - jnp.where(inlet, half, none),
        jnp.where(wall, none, jnp.where(inlet, half, half + half)) - 0.5,
        rate(R_EPS, 1 / 36), rate(R_EPS, 1 / 12), rate(R_NU, 1 / 6), rate(R_NU, 1 / 2),
    ]


def moments(f):
    s = [f[a] + f[b] for a, b in PAIRS]
    d = [f[a] - f[b] for a, b in PAIRS]
    big_s = [s[3] + s[4], s[5] + s[6], s[7] + s[8]]
    off = [s[3] - s[4], s[5] - s[6], s[7] - s[8]]
    ex, gy = d[3] + d[4], d[3] - d[4]
    gx, ez = d[5] + d[6], d[5] - d[6]
    ey, gz = d[7] + d[8], d[7] - d[8]
    return s, d, big_s, off, (ex, ey, ez), (gx, gy, gz)


def even_terms(axis, edge, edge_yz, p1, q1, p2, q2, t):
    a1, b1, a2, b2 = p1 - 2.0 * q1, p1 + q1, p2 - 2.0 * q2, p2 + q2
    xy, xz, yz = edge + b1 + b2, edge + b1 - b2, edge_yz - 2.0 * b1
    return [
        axis[0] + 2.0 * a1, axis[1] - a1 + a2, axis[2] - a1 - a2,
        xy + t[0], xy - t[0], xz + t[1], xz - t[1], yz + t[2], yz - t[2],
    ]


def odd_terms(q, m, along, less):
    base = [q[a] if less[a] is None else q[a] - less[a] for a in range(3)]
    pos, neg = [base[a] + m[a] for a in range(3)], [base[a] - m[a] for a in range(3)]
    return along + [
        pos[0] + neg[1], pos[0] - neg[1], neg[0] + pos[2], neg[0] - pos[2], pos[1] + neg[2], pos[1] - neg[2],
    ]


def turned(f, s, d, zero, sums, diffs, keep, turn):
    out = [None] * 19
    out[0] = 2.0 * (keep * f[0] - zero)
    for n, (a, b) in enumerate(PAIRS):
        even, odd = keep * s[n] - sums[n], turn * d[n] - diffs[n]
        out[a], out[b] = even + odd, even - odd
    return out


def collide_tile(f, coefs):
    c_e, c_eps, c_nu, c_q, c_m, keep, turn, c_eps7, c_eps21, c_nu3, c_nu9 = coefs
    s, d, big, off, e, g = moments(f)
    across = s[1] + s[2]
    axis_sum = s[0] + across
    edge_sum = big[0] + big[1] + big[2]
    rho = f[0] + axis_sum + edge_sum
    eg = [e[a] + g[a] for a in range(3)]
    j = [d[a] + eg[a] for a in range(3)]
    inv = 1.0 / rho
    u = [j[a] * inv for a in range(3)]
    xx, yy, zz = j[0] * u[0], j[1] * u[1], j[2] * u[2]
    beside = yy + zz
    energy = xx + beside
    e1 = c_e * (edge_sum - f[0] - energy)
    e2 = c_eps * (9.0 * f[0] - 7.0 * axis_sum - 2.0 * edge_sum + 5.5 * energy)
    yz_a, yz_e, yz_u = s[1] - s[2], big[0] - big[1], yy - zz
    x_a = 2.0 * s[0] - across
    x_e = big[0] + big[1] - 2.0 * big[2]
    x_u = 2.0 * xx - beside
    p1 = c_nu * (x_a + x_e - x_u)
    q1 = c_eps7 * (x_e - 2.0 * x_a + 0.5 * x_u)
    p2 = c_nu3 * (yz_a + yz_e - yz_u)
    q2 = c_eps21 * (yz_e - 2.0 * yz_a + 0.5 * yz_u)
    c_off = c_nu9
    t = [c_off * (off[0] - j[0] * u[1]), c_off * (off[1] - j[0] * u[2]), c_off * (off[2] - j[1] * u[2])]
    q = [c_q * (eg[a] - 2.0 * d[a]) for a in range(3)]
    m = [c_m * (e[a] - g[a]) for a in range(3)]
    inlet = 0.5 - keep
    axis, edge = -22.0 * e1 - 8.0 * e2, 16.0 * e1 + 2.0 * e2
    zero = 12.0 * e2 - 30.0 * e1 - inlet * (IN_NO / 3)
    axis_yz = axis - inlet * (IN_NO / 9)
    sums = even_terms(
        (axis - inlet * (IN_CX / 9), axis_yz, axis_yz), edge - inlet * (IN_CX / 18), edge - inlet * (IN_NO / 18), p1, q1, p2, q2, t
    )
    along = [-4.0 * q[0] - inlet * (0.15 / 9), -4.0 * q[1], -4.0 * q[2]]
    diffs = odd_terms(q, m, along, (inlet * (0.15 / 18), None, None))
    post = turned(f, s, d, zero, sums, diffs, keep, turn)
    return post, u, [f[OPP[i]] - post[i] for i in range(19)]


def adjoint_tile(b, u, coefs):
    c_e, c_eps, c_nu, c_q, c_m, keep, turn, c_eps7, c_eps21, c_nu3, c_nu9 = coefs
    s, d, big, off, e, g = moments(b)
    across = s[1] + s[2]
    axis_sum = s[0] + across
    edge_sum = big[0] + big[1] + big[2]
    eg = [e[a] + g[a] for a in range(3)]
    e1 = c_e * ((8 / 19) * edge_sum - (11 / 19) * axis_sum - (30 / 19) * b[0])
    e2 = c_eps * (12.0 * b[0] - 4.0 * axis_sum + edge_sum)
    yz_a, yz_e = s[1] - s[2], big[0] - big[1]
    x_a = 2.0 * s[0] - across
    x_e = big[0] + big[1] - 2.0 * big[2]
    p1 = c_nu * (x_a + x_e)
    q1 = c_eps7 * (x_e - 2.0 * x_a)
    p2 = c_nu3 * (yz_a + yz_e)
    q2 = c_eps21 * (yz_e - 2.0 * yz_a)
    c_off = c_nu9
    t = [c_off * off[n] for n in range(3)]
    q = [c_q * (0.6 * eg[a] - 2.4 * d[a]) for a in range(3)]
    m = [c_m * (e[a] - g[a]) for a in range(3)]
    common = 76.0 * e1 - 22.0 * e2
    v, w = 2.0 * p1 - q1, 2.0 * p2 - q2
    less_v = common - v
    k = [common + 2.0 * v, less_v + w, less_v - w]
    gx = k[0] * u[0] + t[0] * u[1] + t[1] * u[2]
    gy = k[1] * u[1] + t[0] * u[0] + t[2] * u[2]
    gz = k[2] * u[2] + t[1] * u[0] + t[2] * u[1]
    by_rho = 6.0 * e2 - 22.0 * e1 - 0.5 * (gx * u[0] + gy * u[1] + gz * u[2])
    by_j = [gx - (2 / 3) * q[0], gy - (2 / 3) * q[1], gz - (2 / 3) * q[2]]
    axis, edge = -22.0 * e1 - 8.0 * e2 - by_rho, 16.0 * e1 + 2.0 * e2 - by_rho
    zero = 12.0 * e2 - 30.0 * e1 - 0.5 * by_rho
    sums = even_terms((axis, axis, axis), edge, edge, p1, q1, p2, q2, t)
    diffs = odd_terms(q, m, [-4.0 * q[a] - by_j[a] for a in range(3)], by_j)
    return turned(b, s, d, zero, sums, diffs, keep, turn)


def dot_gap(b, gap):
    parts = [b[i] * gap[i] for i in range(19)]
    while len(parts) > 1:
        parts = [a + c for a, c in zip(parts[::2], parts[1::2])] + parts[len(parts) // 2 * 2 :]
    return parts[0]


def iota(axis):
    return lax.broadcasted_iota(jnp.int32, (8, LANES), axis)


def pull(load, lane, sense, column, ring, split=False):
    z = lane & (NZ - 1)
    lower = lane < 64

    def shifted(plane, off_x, along_y, amount):
        if split:
            high, low = load(plane, 2, off_x), load(plane, 3, off_x)
            if along_y == 0:
                mixed = jnp.where(lower, high, low)
            elif along_y > 0:
                mixed = jnp.where(lane < 64 - NZ, high, jnp.where(lane < LANES - NZ, low, load(plane, 1, off_x)))
            else:
                mixed = jnp.where(lane < NZ, load(plane, 0, off_x), jnp.where(lane < 64 + NZ, high, low))
        else:
            mixed = load(plane, column, off_x)
            if along_y != 0:
                there = load(plane, (column - along_y) % ring, off_x)
                mixed = jnp.where(lane >= LANES - NZ if along_y > 0 else lane < NZ, there, mixed)
        return pltpu.roll(mixed, amount % LANES, 1) if amount != 0 else mixed

    arrived = []
    for i, (cx, cy, cz) in enumerate(VEL):
        value = shifted(i, -sense * cx, sense * cy, sense * (NZ * cy + cz))
        if cz != 0:
            edge = 0 if sense * cz == 1 else NZ - 1
            value = jnp.where(z == edge, shifted(OPP[i], 0, 0, 0), value)
        arrived.append(value)
    return arrived


def counts(c):
    return (5 - c, 3 + c), (5 + c, 3 - c)


def fold_tables(low, lane):
    tables = {}
    for c in (-1, 0, 1):
        cut = jnp.where(low, NZ * (5 - c), NZ * (3 - c))
        tables[c] = cut, jnp.where(low, lane - cut, cut - 1 - lane) < 0
    return tables


def wall_layers(low):
    where = jnp.where
    return [
        (0, (where(low, 4, 5), where(low, 5, 0))), (1, (where(low, 4, 5), where(low, 6, 1))),
        (2, (where(low, 2, 3), where(low, 7, 2))), (3, (where(low, 2, 3), where(low, 5, 2))),
    ]


def first_kernel(
    snap_hbm, flag_hbm, por_hbm, adj_hbm, post_ref, adj_ref, u_ref, gap_ref, xp_ref, out_ref, in_ref, dg_ref,
    snap_ref, flag_ref, por_ref, sems,
):
    core = lax.rem(lax.axis_index("gy"), 2)
    rows = snap_ref.shape[1]
    lane, row = iota(1), iota(0)
    groups = rows // 8
    order = [0, groups - 1] + list(range(1, groups - 1))
    copies = [(flag_hbm, flag_ref), (por_hbm, por_ref), (adj_hbm, adj_ref)]
    copies += [(snap_hbm.at[:, 8 * g : 8 * g + 8], snap_ref.at[:, 8 * g : 8 * g + 8]) for g in order]
    copies = [pltpu.make_async_copy(src, dst, sems.at[n]) for n, (src, dst) in enumerate(copies)]
    for copy in copies:
        copy.start()
    for copy in copies[:3]:
        copy.wait()

    def collide_rows(g):
        copies[3 + order.index(g)].wait()
        at = slice(8 * g, 8 * g + 8)
        for c in range(2):
            lanes = slice(c * LANES, (c + 1) * LANES)
            kind, porous = flag_ref[at, lanes].astype(F32), por_ref[at, lanes]
            post, u, gap = collide_tile([snap_ref[i, at, lanes] for i in range(19)], coefficients(kind, porous))
            for i, value in enumerate(post + [porous, kind]):
                post_ref[i, at, lanes] = value
            for i in range(19):
                gap_ref[i, at, lanes] = gap[i]
            for a in range(3):
                u_ref[a, at, lanes] = u[a]

    def plane(i, at, lanes):
        return post_ref[i, at, lanes]

    def low_spare(i, at, lanes, axis, where, unit, roll):
        value, first = plane(i, at, lanes), WALL[axis]
        extras = [(post_ref, 0, 4, 5), (post_ref, 1, 4, 6), (adj_ref, 2, 2, 7)] if i == 19 else [(adj_ref, 3, 2, 5)]
        for ref, n, layer, slot in extras:
            moved = roll(ref[first + n, at, lanes], unit * (slot - layer))
            value = jnp.where(where >= unit * slot, moved, value)
        return value

    def high_spare(i, at, lanes, axis, where, unit, roll):
        value, first = plane(i, at, lanes), WALL[axis]
        extras = [(post_ref, 2, 3, 2), (adj_ref, 1, 5, 1), (adj_ref, 0, 5, 0)] if i == 19 else [(post_ref, 3, 3, 2)]
        for ref, n, layer, slot in extras:
            moved = roll(ref[first + n, at, lanes], (unit * (slot - layer)) % (unit * 8))
            value = jnp.where(where < unit * (slot + 1), moved, value)
        return value

    def roll_rows(value, amount):
        return pltpu.roll(value, amount, 0)

    def roll_lanes(value, amount):
        return pltpu.roll(value, amount, 1)

    first_core = core == 0

    def pack_rows(g):
        at = slice(8 * g, 8 * g + 8)
        left, right = slice(0, LANES), slice(LANES, 2 * LANES)
        for i in range(21):
            if i < 19:
                (n, _), (_, m) = counts(VEL[i][1])
                low = jnp.where(lane < NZ * n, plane(i, at, left), pltpu.roll(adj_ref[i, at, left], NZ * n, 1))
                high = jnp.where(lane >= NZ * m, plane(i, at, right), pltpu.roll(adj_ref[i, at, right], NZ * m, 1))
            else:
                low = low_spare(i, at, left, 1, lane, NZ, roll_lanes)
                high = high_spare(i, at, right, 1, lane, NZ, roll_lanes)
            out_ref[i, at, :] = jnp.where(first_core, low, high)
            in_ref[i, at, :] = jnp.where(first_core, high, low)

    for g in order[:2]:
        collide_rows(g)
        pack_rows(g)
    low_rows, high_rows = slice(0, 8), slice(rows - 8, rows)
    spare_rows, walls = [None] * 5, []
    folds = fold_tables(core == 0, lane)
    for i in range(21):
        lows, highs = [], []
        for c in range(2):
            lanes = slice(c * LANES, (c + 1) * LANES)
            if i < 19:
                (n_low, _), (_, m_high) = counts(VEL[i][0])
                low, high = plane(i, low_rows, lanes), plane(i, high_rows, lanes)
                low = jnp.where(row < n_low, low, pltpu.roll(adj_ref[i, low_rows, lanes], n_low, 0))
                high = jnp.where(row >= m_high, high, pltpu.roll(adj_ref[i, high_rows, lanes], m_high, 0))
            else:
                low = low_spare(i, low_rows, lanes, 0, row, 1, roll_rows)
                high = high_spare(i, high_rows, lanes, 0, row, 1, roll_rows)
            xp_ref[0, i, :, lanes] = low
            xp_ref[1, i, :, lanes] = high
            lows.append(low)
            highs.append(high)
        low, high = jnp.where(core == 0, *lows), jnp.where(core == 0, *highs)
        if len(dg_ref.shape) == 4:
            dg_ref[0, i], dg_ref[1, i] = low, high
        elif i >= 19:
            for n, (layer, slot) in wall_layers(core == 0):
                if (n == 3) == (i == 20):
                    kept = [pltpu.roll(t, (NZ * (slot - layer)) % LANES, 1) for t in walls[n]]
                    low, high = [jnp.where(lane // NZ == slot, k, t) for k, t in zip(kept, (low, high))]
            dg_ref[i], dg_ref[i + 2] = low, high
        else:
            if i >= WALL[1]:
                walls.append((low, high))
            cut, collided = folds[VEL[i][1]]
            own = jnp.where(row < n_low, low, high)
            other = jnp.where(row < n_low - 2, high, low)
            dg_ref[i] = jnp.where(collided, own, pltpu.roll(other, cut, 1))
            slot = 2 * (i % 4)
            moved = pltpu.roll(high, (slot - n_low + 2) % 8, 0)
            spare_rows[i // 4] = moved if slot == 0 else jnp.where(row < slot, spare_rows[i // 4], moved)
    if len(dg_ref.shape) == 3:
        for n in range(5):
            dg_ref[23 + n] = spare_rows[n]
    for g in order[2:]:
        collide_rows(g)
        pack_rows(g)


def second_kernel(
    post_in, adj_in, u0_ref, gap0_ref, xr, out_in, in_in, dg_in, xin, res_hbm, sens_hbm,
    p0, p1, p2, pe, cf, u1, u2, u3, g1, g2, g3, a4, a3, a2, a1, s1, s2, s3, res_ref, sens_ref, sems,
):
    first_core = lax.rem(lax.axis_index("gy"), 2) == 0
    rows = post_in.shape[1]
    groups = rows // 8
    lane = iota(1)
    lower = lane < 64
    roll_lanes = lambda value, amount: pltpu.roll(value, amount % LANES, 1)
    roll_rows = lambda value, amount: pltpu.roll(value, amount % 8, 0)

    def beside(i, at):
        out, inside = out_in[i, at], in_in[i, at]
        return jnp.where(first_core, inside, out), jnp.where(first_core, out, inside)

    row = iota(0)
    folds = fold_tables(jnp.logical_not(first_core), lane)
    walls = wall_layers(jnp.logical_not(first_core))

    def outer_corner(side, i):
        if len(dg_in.shape) == 4:
            return dg_in[side, i]
        if i >= 19:
            return dg_in[i + 2 * side]
        tile, n = dg_in[i], 5 - VEL[i][0]
        other = pltpu.roll(tile, LANES - folds[VEL[i][1]][0], 1)
        if side == 0:
            tile = jnp.where(row < n, tile, other)
        else:
            spare = roll_rows(dg_in[23 + i // 4], n - 2 - 2 * (i % 4))
            tile = jnp.where(row >= n, tile, jnp.where(row >= n - 2, spare, other))
        if i >= WALL[1]:
            n, (layer, slot) = walls[i - WALL[1]]
            kept = pltpu.roll(dg_in[(20 if n == 3 else 19) + 2 * side], (NZ * (layer - slot)) % LANES, 1)
            tile = jnp.where(lane // NZ == layer, kept, tile)
        return tile

    def corner(side, i):
        out, near, far = outer_corner(side, i), xin[side, i, :, 0:LANES], xin[side, i, :, LANES:]
        return jnp.where(first_core, near, out), jnp.where(first_core, out, far)

    top, bottom = slice(8 + rows, 16 + rows), slice(0, 8)
    for g in range(groups):
        at, to = slice(8 * g, 8 * g + 8), slice(8 + 8 * g, 16 + 8 * g)
        spare = {}
        for i in (19, 20) + tuple(range(19)):
            high, low = beside(i, at)
            if i >= 19:
                spare[i] = (high, low)
                pe[i - 19, to] = jnp.where(lower, high, low)
            p0[i, 0, to] = post_in[i, at, 0:LANES]
            p0[i, 1, to] = post_in[i, at, LANES:]
            n = i - WALL[1]
            p0[i, 2, to] = jnp.where(lower, high, roll_lanes(spare[19][0], -NZ * (1 + n))) if n in (0, 1) else high
            p0[i, 3, to] = jnp.where(lower, roll_lanes(spare[17 + n][1], NZ), low) if n in (2, 3) else low
            if i < 19:
                (n_low, _), (_, m_high) = counts(VEL[i][1])
                high, low = roll_lanes(high, -NZ * n_low), roll_lanes(low, -NZ * m_high)
                if n in (0, 1):
                    low = jnp.where(lane >= 96, low, roll_lanes(spare[19][1], NZ * (5 - n)))
                if n in (2, 3):
                    high = jnp.where(lane < 32, high, roll_lanes(spare[17 + n][0], -NZ * ((7, 5)[n - 2] - 2)))
                a4[i, 0, to] = adj_in[i, at, 0:LANES]
                a4[i, 1, to] = adj_in[i, at, LANES:]
                a4[i, 2, to] = jnp.where(lower, high, low)
    for side, to in ((0, top), (1, bottom)):
        for i in range(21):
            high, low = corner(side, i)
            tile = [xr[side, i, :, 0:LANES], xr[side, i, :, LANES:], high, low]
            edge = jnp.where(lower, high, low)
            for c in range(4):
                p0[i, c, to] = tile[c]
            if i >= 19:
                pe[i - 19, to] = edge
                continue
            (n_low, _), (_, m_high) = counts(VEL[i][0])
            for c, value in enumerate((tile[0], tile[1], edge)):
                a4[i, c, to] = roll_rows(value, -n_low if side == 0 else -m_high)
    moves = [(p0, 0, 19, 8 + rows + 5, 8 + rows + 4), (p0, 1, 19, 8 + rows + 6, 8 + rows + 4)]
    moves += [(a4, 2, 19, 8 + rows + 7, 8 + rows + 2), (a4, 3, 20, 8 + rows + 5, 8 + rows + 2)]
    moves += [(a4, 0, 19, 0, 5), (a4, 1, 19, 1, 5), (p0, 2, 19, 2, 3), (p0, 3, 20, 2, 3)]
    for dst, n, src, row, to in moves:
        for c in range(4):
            if dst is p0:
                dst[WALL[0] + n, c, to : to + 1] = p0[src, c, row : row + 1]
            elif c < 3:
                dst[WALL[0] + n, c, to : to + 1] = pe[src - 19, row : row + 1] if c == 2 else p0[src, c, row : row + 1]

    def fill(k, carry):
        at = pl.ds(pl.multiple_of(8 * k, 8), 8)
        for c in range(4):
            for n, value in enumerate(coefficients(p0[20, c, at], p0[19, c, at])):
                cf[n, c, at] = value
        for n in range(11):
            cf[n, 4, at] = jnp.where(lower, cf[n, 2, at], cf[n, 3, at])
        return carry

    lax.fori_loop(0, groups + 2, fill, 0, unroll=True)

    def kinds(c, cells, ring):
        column = 4 if ring == 3 and c == 2 else c
        return [cf[n, column, cells] for n in range(11)]

    def forward(src, src_base, base, n_groups, src_ring, ring, post_dst, u_dst, gap_dst):
        def body(k, carry):
            def load(i, c, off):
                return src[i, c, pl.ds(8 * k + (base - src_base + off), 8)]

            at = pl.ds(pl.multiple_of(8 * k, 8), 8)
            cells = pl.ds(8 * k + (base + 8), 8)
            sides = []
            for c in range(ring):
                f = pull(load, lane, 1, c, src_ring, src_ring != ring and c == 2)
                post, u, gap = collide_tile(f, kinds(c, cells, ring))
                if post_dst is not None:
                    for i in range(19):
                        post_dst[i, c, at] = post[i]
                if c < 2:
                    for i in range(19):
                        gap_dst[i, c, at] = gap[i]
                elif ring == 4:
                    sides.append(u)
                    if c == 2:
                        continue
                    u, c = [jnp.where(lower, a, b) for a, b in zip(*sides)], 2
                for a in range(3):
                    u_dst[a, c, at] = u[a]
            return carry

        lax.fori_loop(0, n_groups, body, 0, unroll=True)

    forward(p0, -8, -5, groups + 2, 4, 4, p1, u1, g1)
    forward(p1, -5, -4, groups + 1, 4, 3, p2, u2, g2)
    forward(p2, -4, -3, groups + 1, 3, 3, None, u3, g3)

    def backward(src, src_base, base, dst, u_src, gap_src, f_base, s_dst):
        def body(k, carry):
            def load(i, c, off):
                return src[i, c, pl.ds(8 * k + (base - src_base + off), 8)]

            at = pl.ds(pl.multiple_of(8 * k, 8), 8)
            cells = pl.ds(8 * k + (base + 8), 8)
            old = pl.ds(8 * k + (base - f_base), 8)
            for c in range(3):
                b = pull(load, lane, -1, c, 3)
                if c < 2:
                    s_dst[c, at] = dot_gap(b, [gap_src[i, c, old] for i in range(19)])
                a = adjoint_tile(b, [u_src[n, c, old] for n in range(3)], kinds(c, cells, 3))
                for i in range(19):
                    dst[i, c, at] = a[i]
            return carry

        lax.fori_loop(0, groups + 1, body, 0, unroll=True)

    backward(a4, -8, -3, a3, u3, g3, -3, s3)
    backward(a3, -3, -2, a2, u2, g2, -4, s2)
    backward(a2, -2, -1, a1, u1, g1, -5, s1)

    def results(k):
        at = pl.ds(pl.multiple_of(8 * k, 8), 8)
        return pltpu.make_async_copy(res_ref.at[:, at], res_hbm.at[:, at], sems.at[k])

    def last(k, carry):
        at = pl.ds(pl.multiple_of(8 * k, 8), 8)

        def load(i, c, off):
            return a1[i, c, pl.ds(8 * k + (1 + off), 8)]

        for c in range(2):
            lanes = slice(c * LANES, (c + 1) * LANES)
            b = pull(load, lane, -1, c, 3)
            total = dot_gap(b, [gap0_ref[i, at, lanes] for i in range(19)])
            later = s3[c, pl.ds(8 * k + 3, 8)] + s2[c, pl.ds(8 * k + 2, 8)] + s1[c, pl.ds(8 * k + 1, 8)]
            sens_ref[at, lanes] = (total + later) / (1.0 - post_in[19, at, lanes])
            a = adjoint_tile(b, [u0_ref[n, at, lanes] for n in range(3)], kinds(c, pl.ds(pl.multiple_of(8 * k + 8, 8), 8), 3))
            for i in range(19):
                res_ref[i, at, lanes] = a[i]
        results(k).start()
        return carry

    lax.fori_loop(0, groups, last, 0, unroll=True)
    sens_copy = pltpu.make_async_copy(sens_ref, sens_hbm, sems.at[groups])
    sens_copy.start()
    for k in range(groups):
        results(k).wait()
    sens_copy.wait()


VMEM = pl.BlockSpec(memory_space=pltpu.VMEM)
HBM = pl.BlockSpec(memory_space=pltpu.HBM)


def exchange(xp, out, inside, dg):
    nx, ny = lax.axis_size("gx"), lax.axis_size("gy")
    same = [(i, i ^ 1) for i in range(ny)]
    other = [(i, (i + 1) % ny if i % 2 else (i - 1) % ny) for i in range(ny)]

    def along(value, axes, pairs_of):
        if nx == 2:
            return lax.ppermute(value, axes, pairs_of(1))
        return jnp.stack([lax.ppermute(value[0], axes, pairs_of(-1)), lax.ppermute(value[1], axes, pairs_of(1))])

    xr = along(xp, "gx", lambda step: [(i, (i + step) % nx) for i in range(nx)])
    out_r = lax.ppermute(out, "gy", other)
    dg_r = along(
        dg, ("gx", "gy"), lambda step: [(i * ny + j, ((i + step) % nx) * ny + k) for i in range(nx) for j, k in other]
    )
    in_r = lax.ppermute(inside, "gy", same)
    xr, out_r, dg_r, in_r = lax.optimization_barrier((xr, out_r, dg_r, in_r))
    xin = lax.ppermute(xr, "gy", same)
    return xr, out_r, in_r, dg_r, xin


def per_device(snapshot, flags, porosity, adjoint_end):
    _, rows, lanes = snapshot.shape
    assert lanes == 2 * LANES and rows % 8 == 0

    def array(*shape):
        return jax.ShapeDtypeStruct(shape, F32)

    def scratch(*shape):
        return pltpu.VMEM(shape, F32)

    groups = rows // 8
    post, adj, u0, gap0, xp, out, inside, dg = pl.pallas_call(
        first_kernel,
        out_shape=(
            array(21, rows, lanes), array(19, rows, lanes), array(3, rows, lanes), array(19, rows, lanes),
            array(2, 21, 8, lanes), array(21, rows, LANES), array(21, rows, LANES),
            array(*((28,) if lax.axis_size("gx") == 2 else (2, 21)), 8, LANES),
        ),
        in_specs=[HBM] * 4,
        out_specs=(VMEM,) * 8,
        scratch_shapes=[
            scratch(19, rows, lanes), pltpu.VMEM((rows, lanes), jnp.int32), scratch(rows, lanes),
            pltpu.SemaphoreType.DMA((groups + 3,)),
        ],
        compiler_params=pltpu.CompilerParams(vmem_limit_bytes=12 << 20),
        name="collide_and_pack",
    )(*[pltpu.with_memory_space_constraint(v, pltpu.HBM) for v in (snapshot, flags, porosity, adjoint_end)])
    received = exchange(xp, out, inside, dg)
    tall, mid = rows + 24, rows + 16
    return pl.pallas_call(
        second_kernel,
        out_shape=(array(19, rows, lanes), array(rows, lanes)),
        in_specs=[VMEM] * 9,
        out_specs=(HBM, HBM),
        scratch_shapes=[
            scratch(21, 4, tall, LANES), scratch(19, 4, tall, LANES), scratch(19, 3, tall, LANES), scratch(2, tall, LANES),
            scratch(11, 5, tall, LANES),
            scratch(3, 3, mid, LANES), scratch(3, 3, mid, LANES), scratch(3, 3, mid, LANES),
            scratch(19, 2, mid, LANES), scratch(19, 2, mid, LANES), scratch(19, 2, mid, LANES),
            scratch(19, 3, mid, LANES), scratch(19, 3, mid, LANES), scratch(19, 3, mid, LANES), scratch(19, 3, mid, LANES),
            scratch(2, mid, LANES), scratch(2, mid, LANES), scratch(2, mid, LANES),
            scratch(19, rows, lanes), scratch(rows, lanes), pltpu.SemaphoreType.DMA((groups + 1,)),
        ],
        compiler_params=pltpu.CompilerParams(vmem_limit_bytes=28 << 20),
        name="window",
    )(post, adj, u0, gap0, *received)


def solution(mesh):
    placed = (P(None, "gx", "gy"), P("gx", "gy"), P("gx", "gy"), P(None, "gx", "gy"))
    return jax.shard_map(
        per_device,
        mesh=mesh,
        in_specs=placed,
        out_specs=(P(None, "gx", "gy"), P("gx", "gy")),
        check_vma=False,
    )
```
